32 devices in a mesh: gx: 8 (over z, y), gy: 4 (over x, core).
Axes of the slice: x: 2, y: 2, z: 4, core: 2. Of those that a mesh axis runs over, the one named last changes fastest.
Arguments:
- positions: float32 [3, 8, 4, 256], P(None, 'gx', 'gy'), may hold values from 0 to 22
- features: bfloat16 [8, 4, 256, 256], P('gx', 'gy'), may hold values from -6 to 6
- species: int32 [8, 4, 256], P('gx', 'gy'), may hold values from 0 to 1
- atom_count: int32 [8, 4], P('gx', 'gy'), may hold values from 128 to 256, as said below
- quad_list: int32 [8, 4, 2, 2, 64], P('gx', 'gy'), may hold values from -1 to 255, as said below
- tile_pairs: int32 [8, 4, 8, 2], P('gx', 'gy'), may hold values from -1 to 15, as said below
- w_up: bfloat16 [256, 256], replicated, may hold values from -0.375 to 0.375
- w_radial: float32 [8, 3, 256], replicated, may hold values from -5 to 5
- w_mix: bfloat16 [3, 256, 256], replicated, may hold values from -0.375 to 0.375
- w_prod: bfloat16 [4, 256, 256], replicated, may hold values from -0.1875 to 0.1875
- w_read: float32 [256], replicated, may hold values from -1.5 to 1.5
- e_ref: float32 [2], replicated, may hold values from -4 to 4
Outputs:
- energies: float32 [8, 4, 256], P('gx', 'gy')
- forces: float32 [3, 8, 4, 256], P(None, 'gx', 'gy')
- feature_grad: float32 [8, 4, 256, 256], P('gx', 'gy')
The draws below stay inside these ranges and needn't reach their ends.
Inputs may be any that keep to these rules, and one draw needn't show every extreme that they name: `atom_count`: each device holds at least 128 and at most 256 atoms; at least one device is full with 256. `quad_list`: first index: lower or upper half of the domain along x, second: along y. Every slot below the device's atom_count appears exactly once in the device's four lists, -1 marks an empty entry, and on a full device no entry is empty. `tile_pairs`: per device, pairs (owned tile, extended tile); the pairs are distinct, the live ones come first, -1 fills both entries of the others; every device has at least 2 live pairs and some device has 8. A domain is 10 x 10 angstrom in x and y; owned tile t holds the atoms with z between 5.5 t and 5.5 (t + 1), a quadrant list the atoms of one 5 x 5 angstrom quarter of the domain; live pairs are only pairs of tiles whose atoms may lie within the cutoff of each other.
All inputs are finite; a program needn't handle non-finite values.
Results may differ from the reference program's by a relative error of at most 0.01.
Values may be sent and summed in bfloat16 or wider, within the bound.
A program may use at most 64 MiB of HBM per device.

```python
import jax
import jax.numpy as jnp
from jax import lax

C = 256
BASIS = 8
TILE = 64
OWN_TILES = 4
ATOMS_DEV = 256
QUAD = 64
PAIRS = 8
GRID_X = 8
GRID_Y = 4


border_reach = 1.5


def atom_layout(key):
    devices = GRID_X * GRID_Y
    counts = jax.random.randint(jax.random.fold_in(key, 101), (devices,), ATOMS_DEV // 2, ATOMS_DEV + 1)
    fullest = jax.random.randint(jax.random.fold_in(key, 102), (), 0, devices)
    counts = jnp.where(jnp.arange(devices) == fullest, ATOMS_DEV, counts).astype(jnp.int32)
    perm_keys = jax.random.split(jax.random.fold_in(key, 103), devices)
    orders = jax.vmap(lambda single: jax.random.permutation(single, ATOMS_DEV))(perm_keys).astype(jnp.int32)
    return (counts, orders)


def draw_atom_count(key, part):
    counts, orders = atom_layout(key)
    return counts.reshape(GRID_X, GRID_Y)


def draw_quad_list(key, part):
    counts, orders = atom_layout(key)
    lists = jnp.where(orders < counts[:, None], orders, -1)
    return lists.reshape(GRID_X, GRID_Y, 2, 2, QUAD).astype(jnp.int32)


def draw_positions(key, part):
    counts, orders = atom_layout(key)
    slots = jnp.arange(ATOMS_DEV, dtype=jnp.int32)
    places = jax.vmap(lambda order: jnp.zeros(ATOMS_DEV, jnp.int32).at[order].set(slots))(orders)
    quadrant = places // QUAD
    half_x = (quadrant // 2).astype(jnp.float32)
    half_y = (quadrant % 2).astype(jnp.float32)
    band = (slots // TILE).astype(jnp.float32)[None, :]
    unit = jax.random.uniform(jax.random.fold_in(key, 104), (3, GRID_X * GRID_Y, ATOMS_DEV), jnp.float32)
    coord_x = 10.0 * half_x + (1.0 - 2.0 * half_x) * border_reach * unit[0]
    coord_y = 10.0 * half_y + (1.0 - 2.0 * half_y) * border_reach * unit[1]
    coord_z = (band + unit[2]) * 5.5
    stacked = jnp.stack([coord_x, coord_y, coord_z])
    return stacked.reshape(3, GRID_X, GRID_Y, ATOMS_DEV).astype(jnp.float32)


def draw_tile_pairs(key, part):
    devices = GRID_X * GRID_Y
    per_cell = QUAD // TILE
    device_ids = jnp.arange(devices, dtype=jnp.int32)
    fullest = jax.random.randint(jax.random.fold_in(key, 203), (), 0, devices)
    corner_cells = jnp.array([0, 3, 8, 11], jnp.int32)
    face_cells = jnp.array([1, 2, 4, 5, 6, 7, 9, 10], jnp.int32)
    corner_pick = corner_cells[jax.random.randint(jax.random.fold_in(key, 201), (devices,), 0, 4)]
    corner_pick = jnp.where(device_ids == fullest, 11, corner_pick)
    face_pick = face_cells[jax.random.randint(jax.random.fold_in(key, 204), (devices,), 0, 8)]
    within = jax.random.randint(jax.random.fold_in(key, 205), (2, devices), 0, per_cell)
    first_sub = jnp.where(device_ids == fullest, per_cell - 1, within[0])
    first_tile = OWN_TILES + corner_pick * per_cell + first_sub
    second_tile = OWN_TILES + face_pick * per_cell + within[1]
    order_keys = jax.random.split(jax.random.fold_in(key, 206), devices)
    own_order = jax.vmap(lambda single: jax.random.permutation(single, OWN_TILES))(order_keys).astype(jnp.int32)
    target_all = jnp.concatenate([own_order, own_order], axis=1)
    source_all = jnp.concatenate([jnp.broadcast_to(first_tile[:, None], (devices, OWN_TILES)), jnp.broadcast_to(second_tile[:, None], (devices, OWN_TILES))], axis=1)
    levels = jax.random.randint(jax.random.fold_in(key, 202), (devices,), 0, PAIRS)
    counts = 2 + levels * levels * (PAIRS - 2) // ((PAIRS - 1) * (PAIRS - 1))
    counts = jnp.where(device_ids == fullest, PAIRS, counts)
    live = jnp.arange(PAIRS)[None, :] < counts[:, None]
    target = jnp.where(live, target_all, -1)
    source = jnp.where(live, source_all, -1)
    return jnp.stack([target, source], axis=-1).reshape(GRID_X, GRID_Y, PAIRS, 2).astype(jnp.int32)


def plant(drawn, stream_key, smallest, top_value):
    longest = drawn.shape.index(max(drawn.shape))
    spots = []
    for shift in (0, 1):
        where = [jax.random.randint(jax.random.fold_in(stream_key, axis), (), 0, length) for axis, length in enumerate(drawn.shape)]
        where[longest] = (where[longest] + shift) % drawn.shape[longest]
        spots.append(tuple(where))
    return drawn.at[spots[0]].set(smallest).at[spots[1]].set(top_value)


def block_scale(stream_key, extent, pieces, least, top_value):
    level = 1.0
    for dim, blocks in pieces:
        draws = jax.random.uniform(jax.random.fold_in(jax.random.fold_in(stream_key, 6), dim), (blocks,), jnp.float32, least / len(pieces), top_value / len(pieces))
        level = level * jnp.repeat(jnp.exp(draws), extent[dim] // blocks).reshape((-1,) + (1,) * (len(extent) - 1 - dim))
    return level


def bell_draw(own_key, extent, scale, most, pieces=(), kind=jnp.bfloat16):
    drawn = jax.random.normal(own_key, extent, jnp.float32) * scale
    if len(pieces) > 0:
        drawn = block_scale(own_key, extent, pieces, -0.22, 0.18) * drawn
    return jnp.clip(drawn, min=-most, max=most).astype(kind)


def setup_inputs(seed: int = 0) -> dict:
    splits = jax.random.split(jax.random.key(seed), 13)
    return {
        "positions": draw_positions(jax.random.fold_in(splits[12], 71), 0),
        "features": bell_draw(splits[1], (GRID_X, GRID_Y, ATOMS_DEV, C), 1.0, 6.0, ((0, 8), (1, 4))),
        "species": plant(jax.random.randint(splits[2], (GRID_X, GRID_Y, ATOMS_DEV), 0, 2), jax.random.fold_in(splits[2], 1), 0, 1).astype(jnp.int32),
        "atom_count": draw_atom_count(jax.random.fold_in(splits[12], 71), 0),
        "quad_list": draw_quad_list(jax.random.fold_in(splits[12], 71), 0),
        "tile_pairs": draw_tile_pairs(jax.random.fold_in(splits[12], 71), 0),
        "w_up": bell_draw(splits[6], (C, C), C ** -0.5, 0.375),
        "w_radial": bell_draw(splits[7], (BASIS, 3, C), 1.0, 5.0, (), jnp.float32),
        "w_mix": bell_draw(splits[8], (3, C, C), C ** -0.5, 0.375),
        "w_prod": bell_draw(splits[9], (4, C, C), (4 * C) ** -0.5, 0.1875),
        "w_read": bell_draw(splits[10], (C,), 0.25, 1.5, (), jnp.float32),
        "e_ref": bell_draw(splits[11], (2,), 1.0, 4.0, (), jnp.float32),
    }


cutoff_radius = 5.0
domain_width = 10.0
basis_sharpness = 10.0
message_scale = 0.25
degree_limits = ((0, 1), (1, 4), (4, 9))

def rounded(values):
    return lax.optimization_barrier(values.astype(jnp.bfloat16)).astype(jnp.float32)

def harmonics(scaled, squared):
    root_three = 3.0 ** 0.5
    root_five = 5.0 ** 0.5
    root_fifteen = 15.0 ** 0.5
    coord_x = scaled[0]
    coord_y = scaled[1]
    coord_z = scaled[2]
    return jnp.stack([jnp.ones_like(squared), root_three * coord_x, root_three * coord_y, root_three * coord_z, root_fifteen * coord_x * coord_y, root_fifteen * coord_y * coord_z, 0.5 * root_five * (3.0 * coord_z * coord_z - squared), root_fifteen * coord_x * coord_z, 0.5 * root_fifteen * (coord_x * coord_x - coord_y * coord_y)])

def pair_geometry(pos_left, pos_right, pair_mask):
    scaled = (pos_right[:, None, :] - pos_left[:, :, None]) / cutoff_radius
    squared = lax.optimization_barrier(jnp.sum(scaled * scaled, axis=0))
    envelope = jnp.maximum(1.0 - squared, 0.0) ** 3
    centers = jnp.arange(BASIS).astype(pos_left.dtype) / (BASIS - 1)
    radial = (pair_mask * envelope)[None] * jnp.exp(-basis_sharpness * (squared[None] - centers[:, None, None]) ** 2)
    angular = harmonics(scaled, squared)
    joined = angular[:, :, None, :] * jnp.transpose(radial, (1, 0, 2))[None]
    return joined.reshape(9, pos_left.shape[1], BASIS * pos_right.shape[1])

def border_cells():
    listing = []
    for cell_row in range(4):
        for cell_col in range(4):
            if cell_row in (0, 3) or cell_col in (0, 3):
                listing.append((cell_row, cell_col))
    return listing

def cell_anchor(place):
    if place == 0:
        return (-1, 1)
    if place == 3:
        return (1, 0)
    return (0, place - 1)

def add_columns(table, update, first):
    current = lax.dynamic_slice_in_dim(table, first, update.shape[1], 1)
    return lax.dynamic_update_slice_in_dim(table, current + update, first, 1)

def add_rows(table, update, first):
    current = lax.dynamic_slice_in_dim(table, first, update.shape[0], 0)
    return lax.dynamic_update_slice_in_dim(table, current + update, first, 0)

def device_work(ext_pos, ext_valid, ext_hu, pair_list, species_row, w_radial, w_mix, w_prod, w_read, e_ref):
    own_rows = species_row.shape[0]
    channels = ext_hu.shape[1]
    live_pairs = jnp.sum((pair_list[:, 0] >= 0).astype(jnp.int32))
    own_valid = ext_valid[:own_rows]
    radial_weights = w_radial.astype(jnp.float32)

    def pair_inputs(pair_num):
        target = pair_list[pair_num, 0]
        source = pair_list[pair_num, 1]
        start_left = (target * TILE).astype(jnp.int32)
        start_right = (source * TILE).astype(jnp.int32)
        pos_left = lax.dynamic_slice_in_dim(ext_pos, start_left, TILE, 1)
        pos_right = lax.dynamic_slice_in_dim(ext_pos, start_right, TILE, 1)
        valid_left = lax.dynamic_slice_in_dim(ext_valid, start_left, TILE, 0)
        valid_right = lax.dynamic_slice_in_dim(ext_valid, start_right, TILE, 0)
        same_slot = jnp.where(target == source, jnp.eye(TILE, dtype=jnp.float32), jnp.zeros((TILE, TILE), jnp.float32))
        pair_mask = valid_left[:, None] * valid_right[None, :] * (1.0 - same_slot)
        hu_right = lax.dynamic_slice_in_dim(ext_hu, start_right, TILE, 0).astype(jnp.float32)
        weighted_terms = rounded(radial_weights[:, None, :, :] * hu_right[None, :, None, :])
        weighted_terms = weighted_terms.reshape(BASIS * TILE, 3, channels)
        return (start_left, start_right, pos_left, pos_right, pair_mask, weighted_terms)

    def forward_step(pair_num, running):
        start_left, start_right, pos_left, pos_right, pair_mask, weighted_terms = pair_inputs(pair_num)
        second_geometry = rounded(pair_geometry(pos_left, pos_right, pair_mask))
        contribution = jnp.concatenate([jnp.einsum('skx,xd->ksd', second_geometry[lower_order:upper_order], weighted_terms[:, harmonic_degree, :]) for harmonic_degree, (lower_order, upper_order) in enumerate(degree_limits)], axis=1)
        return add_rows(running, contribution, start_left)
    summed = lax.fori_loop(0, live_pairs, forward_step, jnp.zeros((own_rows, 9, channels), jnp.float32))
    contracted_b = rounded(message_scale * summed)
    mix_weights = w_mix.astype(jnp.float32)
    prod_weights = w_prod.astype(jnp.float32)
    mixed = jnp.concatenate([jnp.einsum('amc,cd->amd', contracted_b[:, lower_order:upper_order], mix_weights[harmonic_degree]) for harmonic_degree, (lower_order, upper_order) in enumerate(degree_limits)], axis=1)
    scalar_part = mixed[:, 0]
    first_sq = lax.optimization_barrier(jnp.sum(mixed[:, 1:4] ** 2, axis=1))
    second_sq = lax.optimization_barrier(jnp.sum(mixed[:, 4:9] ** 2, axis=1))
    products_b = rounded(jnp.stack([scalar_part, first_sq, second_sq, scalar_part * first_sq], axis=1))
    message = jnp.einsum('aqc,qcd->ad', products_b, prod_weights)
    gate = jax.nn.sigmoid(message)
    energies = own_valid * (e_ref[species_row] + lax.optimization_barrier(jnp.sum(message * gate * w_read[None, :], axis=1)))
    grad_message = rounded(own_valid[:, None] * w_read[None, :] * gate * (1.0 + message * (1.0 - gate)))
    grad_products = jnp.einsum('ad,qcd->aqc', grad_message, prod_weights)
    grad_zero = grad_products[:, 0] + grad_products[:, 3] * first_sq
    grad_one = 2.0 * mixed[:, 1:4] * (grad_products[:, 1] + grad_products[:, 3] * scalar_part)[:, None, :]
    grad_two = 2.0 * mixed[:, 4:9] * grad_products[:, 2][:, None, :]
    grad_mixed = rounded(jnp.concatenate([grad_zero[:, None, :], grad_one, grad_two], axis=1))
    grad_a = rounded(message_scale * jnp.concatenate([jnp.einsum('amd,cd->amc', grad_mixed[:, lower_order:upper_order], mix_weights[harmonic_degree]) for harmonic_degree, (lower_order, upper_order) in enumerate(degree_limits)], axis=1))

    def backward_step(pair_num, carried):
        grad_pos, grad_hu = carried
        start_left, start_right, pos_left, pos_right, pair_mask, weighted_terms = pair_inputs(pair_num)
        tile_geometry, pullback = jax.vjp(lambda left_pos, right_pos: pair_geometry(left_pos, right_pos, pair_mask), pos_left, pos_right)
        second_geometry = rounded(tile_geometry)
        gradient_rows = lax.dynamic_slice_in_dim(grad_a, start_left, TILE, 0)
        geometry_gradient = jnp.concatenate([jnp.einsum('ebj,kj->bek', gradient_rows[:, lower_order:upper_order], weighted_terms[:, harmonic_degree, :]) for harmonic_degree, (lower_order, upper_order) in enumerate(degree_limits)], axis=0)
        weighted_gradient = jnp.stack([jnp.einsum('vxf,xvp->fp', second_geometry[lower_order:upper_order], gradient_rows[:, lower_order:upper_order]) for harmonic_degree, (lower_order, upper_order) in enumerate(degree_limits)], axis=1)
        grad_source = jnp.einsum('klc,kjlc->jc', radial_weights, weighted_gradient.reshape(BASIS, TILE, 3, channels))
        grad_left, grad_right = pullback(geometry_gradient)
        grad_pos = add_columns(grad_pos, grad_left, start_left)
        grad_pos = add_columns(grad_pos, grad_right, start_right)
        grad_hu = add_rows(grad_hu, grad_source, start_right)
        return (grad_pos, grad_hu)
    ext_rows = ext_hu.shape[0]
    start_grads = (jnp.zeros((3, ext_rows), jnp.float32), jnp.zeros((ext_rows, channels), jnp.float32))
    grad_pos, grad_hu = lax.fori_loop(0, live_pairs, backward_step, start_grads)
    return (energies, grad_pos, grad_hu)

def reference(positions, features, species, atom_count, quad_list, tile_pairs, w_up, w_radial, w_mix, w_prod, w_read, e_ref):
    devices = GRID_X * GRID_Y
    own_pos = jnp.moveaxis(positions, 0, 2)
    own_valid = (jnp.arange(ATOMS_DEV)[None, None, :] < atom_count[:, :, None]).astype(jnp.float32)
    own_hu = jnp.einsum('xyad,dc->xyac', features.astype(jnp.float32), w_up.astype(jnp.float32)).astype(jnp.bfloat16)
    slots = jnp.maximum(quad_list, 0).reshape(GRID_X, GRID_Y, 4 * QUAD).astype(jnp.int32)
    quad_flag = (quad_list >= 0).astype(jnp.float32).reshape(GRID_X, GRID_Y, 4 * QUAD)
    quad_valid = (quad_flag * jnp.take_along_axis(own_valid, slots, axis=2)).reshape(GRID_X, GRID_Y, 2, 2, QUAD)
    quad_pos = jnp.take_along_axis(own_pos, slots[:, :, None, :], axis=3).reshape(GRID_X, GRID_Y, 3, 2, 2, QUAD)
    quad_hu = jnp.take_along_axis(own_hu, slots[:, :, :, None], axis=2).reshape(GRID_X, GRID_Y, 2, 2, QUAD, C)
    listing = border_cells()
    pos_parts = [own_pos]
    valid_parts = [own_valid]
    hu_parts = [own_hu]
    for cell_row, cell_col in listing:
        shift_row, half_row = cell_anchor(cell_row)
        shift_col, half_col = cell_anchor(cell_col)
        offset = jnp.array([shift_row * domain_width, shift_col * domain_width, 0.0]).astype(jnp.float32)
        moved = jnp.roll(quad_pos[:, :, :, half_row, half_col], (-shift_row, -shift_col), axis=(0, 1))
        pos_parts.append(moved + offset[None, None, :, None])
        valid_parts.append(jnp.roll(quad_valid[:, :, half_row, half_col], (-shift_row, -shift_col), axis=(0, 1)))
        hu_parts.append(jnp.roll(quad_hu[:, :, half_row, half_col], (-shift_row, -shift_col), axis=(0, 1)))
    ext_pos = jnp.concatenate(pos_parts, axis=3)
    ext_valid = jnp.concatenate(valid_parts, axis=2)
    ext_hu = jnp.concatenate(hu_parts, axis=2)
    ext_rows = ext_hu.shape[2]

    def work_one(packed):
        return device_work(packed[0], packed[1], packed[2], packed[3], packed[4], w_radial, w_mix, w_prod, w_read, e_ref)
    energies, grad_pos, grad_hu = lax.map(work_one, (ext_pos.reshape(devices, 3, ext_rows), ext_valid.reshape(devices, ext_rows), ext_hu.reshape(devices, ext_rows, C), tile_pairs.reshape(devices, PAIRS, 2), species.reshape(devices, ATOMS_DEV)))
    grad_pos = grad_pos.reshape(GRID_X, GRID_Y, 3, ext_rows)
    grad_hu = grad_hu.reshape(GRID_X, GRID_Y, ext_rows, C)
    back_pos = jnp.zeros((GRID_X, GRID_Y, 2, 2, 3, QUAD), jnp.float32)
    back_hu = jnp.zeros((GRID_X, GRID_Y, 2, 2, QUAD, C), jnp.float32)
    for number, (cell_row, cell_col) in enumerate(listing):
        shift_row, half_row = cell_anchor(cell_row)
        shift_col, half_col = cell_anchor(cell_col)
        first_row = ATOMS_DEV + number * QUAD
        piece_pos = jnp.roll(grad_pos[:, :, :, first_row:first_row + QUAD], (shift_row, shift_col), axis=(0, 1))
        piece_hu = jnp.roll(grad_hu[:, :, first_row:first_row + QUAD], (shift_row, shift_col), axis=(0, 1))
        back_pos = back_pos.at[:, :, half_row, half_col].add(piece_pos)
        back_hu = back_hu.at[:, :, half_row, half_col].add(piece_hu)
    segment = jnp.where(quad_list >= 0, quad_list, ATOMS_DEV).reshape(devices, 4 * QUAD).astype(jnp.int32)
    flat_hu = back_hu.reshape(devices, 4 * QUAD, C)
    flat_pos = jnp.moveaxis(back_pos, 4, 2).reshape(devices, 3, 4 * QUAD)

    def scatter_one(packed):
        gathered_hu = jax.ops.segment_sum(packed[0], packed[2], num_segments=ATOMS_DEV + 1)[:ATOMS_DEV]
        gathered_pos = jax.ops.segment_sum(packed[1].T, packed[2], num_segments=ATOMS_DEV + 1)[:ATOMS_DEV].T
        return (gathered_hu, gathered_pos)
    scattered_hu, scattered_pos = lax.map(scatter_one, (flat_hu, flat_pos, segment))
    total_hu = grad_hu[:, :, :ATOMS_DEV] + scattered_hu.reshape(GRID_X, GRID_Y, ATOMS_DEV, C)
    total_pos = grad_pos[:, :, :, :ATOMS_DEV] + scattered_pos.reshape(GRID_X, GRID_Y, 3, ATOMS_DEV)
    feature_grad = jnp.einsum('xyac,dc->xyad', rounded(total_hu), w_up.astype(jnp.float32))
    forces = jnp.moveaxis(-total_pos, 2, 0)
    return (energies.reshape(GRID_X, GRID_Y, ATOMS_DEV), forces, feature_grad)
```

```python
import functools

import jax
import jax.numpy as jnp
from jax import lax
from jax.experimental import pallas as pl
from jax.experimental.pallas import tpu as pltpu
from jax.sharding import PartitionSpec as P

BASIS = 8
TILE = 64
LANES = 128
GEO = 16

cutoff_radius = 5.0
domain_width = 10.0
basis_sharpness = 10.0
message_scale = 0.25
degree_limits = ((0, 1), (1, 4), (4, 9))
ORDERS = 9
MESH = pl.DeviceIdType.MESH
F32 = jnp.float32
BF16 = jnp.bfloat16
root_three = 3.0**0.5
root_five = 5.0**0.5
root_fifteen = 15.0**0.5


def border_cells():
    return [(r, c) for r in range(4) for c in range(4) if r in (0, 3) or c in (0, 3)]


def cell_anchor(place):
    if place == 0:
        return (-1, 1)
    if place == 3:
        return (1, 0)
    return (0, place - 1)


def cell_table():
    listing = []
    for row, col in border_cells():
        dr, qx = cell_anchor(row)
        dc, qy = cell_anchor(col)
        listing.append((dr, dc, qx, qy))
    return listing


CELLS = cell_table()


def nn(left, right):
    return lax.dot_general(left, right, (((1,), (0,)), ((), ())), preferred_element_type=F32)


def nt(left, right):
    return lax.dot_general(left, right, (((1,), (1,)), ((), ())), preferred_element_type=F32)


def tn(left, right):
    return lax.dot_general(left, right, (((0,), (0,)), ((), ())), preferred_element_type=F32)


def three_parts(row):
    high = row.astype(BF16).astype(F32)
    rest = row - high
    middle = rest.astype(BF16).astype(F32)
    return high, middle, rest - middle


def stack_rows(rows, count, width):
    index = lax.broadcasted_iota(jnp.int32, (count, width), 0)
    out = jnp.zeros((count, width), F32)
    for number, row in enumerate(rows):
        out = jnp.where(index == number, row, out)
    return out


def position_parts(pos_ref):
    rows = []
    for axis in range(3):
        rows.extend(three_parts(pos_ref[axis, 0]))
    return stack_rows(rows, GEO, pos_ref.shape[3]).astype(BF16)


def neighbour(nx, ny, dx, dy):
    return (
        lax.rem(lax.axis_index("gx") + dx + nx, nx),
        lax.rem(lax.axis_index("gy") + dy + ny, ny),
    )


def greet(nx, ny):
    barrier = pltpu.get_barrier_semaphore()
    for dx in (-1, 0, 1):
        for dy in (-1, 0, 1):
            if dx != 0 or dy != 0:
                pl.semaphore_signal(
                    barrier, inc=1, device_id=neighbour(nx, ny, dx, dy), device_id_type=MESH
                )
    return barrier


def halo_kernel(
    nx, ny, count_ref, pos_ref, feat_ref, quad_ref, wup_ref, hu_ref, cells_ref, outbox, send_sem, recv_sem
):
    barrier = greet(nx, ny)
    rows = feat_ref.shape[2]
    channels = feat_ref.shape[3]
    hu = nn(feat_ref[0, 0], wup_ref[...]).astype(BF16)
    hu_ref[...] = hu
    parts = position_parts(pos_ref)
    count = count_ref[0, 0]
    index = lax.broadcasted_iota(jnp.int32, (rows, TILE), 0)
    geo_row = lax.broadcasted_iota(jnp.int32, (GEO, LANES), 0)
    for qx in range(2):
        for qy in range(2):
            slot = quad_ref[0, 0, qx, pl.ds(qy, 1), :]
            hot = (index == slot).astype(F32).astype(BF16)
            quad = 2 * qx + qy
            outbox[quad, 0:TILE, :] = tn(hot, hu).astype(BF16)
            valid = jnp.where((slot >= 0) & (slot < count), 1.0, 0.0)
            geometry = nn(parts, jnp.concatenate([hot, hot], axis=1))
            both = jnp.concatenate([valid, valid], axis=1)
            geometry = jnp.where(geo_row == 9, both, geometry)
            outbox[quad, TILE : TILE + GEO, 0:LANES] = geometry.astype(BF16)
            outbox[quad, TILE : TILE + GEO, LANES:channels] = jnp.zeros((GEO, channels - LANES), BF16)
    pl.semaphore_wait(barrier, 8)
    copies = []
    for number, (dr, dc, qx, qy) in enumerate(CELLS):
        copies.append(
            pltpu.make_async_remote_copy(
                src_ref=outbox.at[2 * qx + qy],
                dst_ref=cells_ref.at[number],
                send_sem=send_sem.at[number],
                recv_sem=recv_sem.at[number],
                device_id=neighbour(nx, ny, -dr, -dc),
                device_id_type=MESH,
            )
        )
        copies[-1].start()
    for copy in copies:
        copy.wait()


def return_kernel(
    nx, ny, msg_ref, own_hu_ref, own_pos_ref, quad_ref, wup_ref, force_ref, grad_ref, inbox, total, send_sem, recv_sem
):
    barrier = greet(nx, ny)
    rows = own_hu_ref.shape[0]
    pl.semaphore_wait(barrier, 8)
    copies = []
    for number, (dr, dc, qx, qy) in enumerate(CELLS):
        copies.append(
            pltpu.make_async_remote_copy(
                src_ref=msg_ref.at[number],
                dst_ref=inbox.at[number],
                send_sem=send_sem.at[number],
                recv_sem=recv_sem.at[number],
                device_id=neighbour(nx, ny, dr, dc),
                device_id_type=MESH,
            )
        )
        copies[-1].start()
    index = lax.broadcasted_iota(jnp.int32, (rows, TILE), 0)
    hots = []
    for qx in range(2):
        for qy in range(2):
            hots.append((index == quad_ref[0, 0, qx, pl.ds(qy, 1), :]).astype(F32).astype(BF16))
    total[...] = own_hu_ref[...]
    shifts = jnp.zeros((GEO, rows), F32)
    for number, (dr, dc, qx, qy) in enumerate(CELLS):
        copies[number].wait()
        hot = hots[2 * qx + qy]
        total[...] += nn(hot, inbox[number, 0:TILE, :])
        shifts = shifts + nt(inbox[number, TILE : TILE + GEO, 0:TILE], hot)
    for axis in range(3):
        force_ref[axis, 0] = -(
            own_pos_ref[axis : axis + 1, :]
            + (shifts[axis : axis + 1, :] + shifts[3 + axis : 4 + axis, :])
        )
    grad_ref[0, 0] = nt(total[...].astype(BF16), wup_ref[...])


def core_kernel(
    pairs_ref,
    count_ref,
    eref_ref,
    pos_ref,
    species_ref,
    hu_ref,
    cells_ref,
    wrad_ref,
    wmix_ref,
    wprod_ref,
    wread_ref,
    energy_ref,
    msg_ref,
    own_hu_ref,
    own_pos_ref,
    hu_tab,
    geo,
    cols,
    hw,
    gb,
    sums,
    mixed,
    prods,
    gprod,
    gmix,
    gat,
    gg,
    ghu,
    gpr,
    gpl,
):
    rows, channels = hu_ref.shape
    own_tiles = rows // TILE
    cells = cells_ref.shape[0]
    tiles = own_tiles + cells
    max_pairs = pairs_ref.shape[2]
    count = count_ref[0, 0]
    live = jnp.int32(0)
    for number in range(max_pairs):
        live = live + jnp.where(pairs_ref[0, 0, number, 0] >= 0, 1, 0)

    parts = position_parts(pos_ref)
    lane = lax.broadcasted_iota(jnp.int32, (1, LANES), 1)
    lane_atom = lax.rem(lane, TILE)
    upper = lane >= TILE
    geo_row = lax.broadcasted_iota(jnp.int32, (8, LANES), 0)

    def set_geometry(tile, raw, valid, shift):
        coords = []
        for axis in range(3):
            first = 3 * axis
            whole = (
                raw[first : first + 1, :] + raw[first + 1 : first + 2, :]
            ) + raw[first + 2 : first + 3, :]
            coords.append(whole + shift[axis])
        geo[tile] = stack_rows(coords + [valid], 8, LANES)

    square = lax.broadcasted_iota(jnp.int32, (rows, LANES), 0)
    for tile in range(own_tiles):
        hu_tab[tile] = hu_ref[tile * TILE : (tile + 1) * TILE, :]
        slot = lane_atom + tile * TILE
        hot = (square == slot).astype(F32).astype(BF16)
        set_geometry(tile, nn(parts, hot), jnp.where(slot < count, 1.0, 0.0), (0.0, 0.0, 0.0))
    for number, (dr, dc, qx, qy) in enumerate(CELLS):
        hu_tab[own_tiles + number] = cells_ref[number, 0:TILE, :]
        raw = cells_ref[number, TILE : TILE + GEO, 0:LANES].astype(F32)
        set_geometry(
            own_tiles + number, raw, raw[9:10, :], (dr * domain_width, dc * domain_width, 0.0)
        )
    eye = (
        lax.broadcasted_iota(jnp.int32, (rows, rows), 0)
        == lax.broadcasted_iota(jnp.int32, (rows, rows), 1)
    ).astype(F32).astype(BF16)
    columns = nt(eye, parts)
    for axis in range(3):
        first = 3 * axis
        whole = (columns[:, first : first + 1] + columns[:, first + 1 : first + 2]) + columns[
            :, first + 2 : first + 3
        ]
        cols[axis] = jnp.broadcast_to(whole, (rows, LANES))
    sums[...] = jnp.zeros_like(sums)
    ghu[...] = jnp.zeros_like(ghu)
    gpr[...] = jnp.zeros_like(gpr)
    gpl[...] = jnp.zeros_like(gpl)

    def scene(target, source, first, height):
        start = pl.multiple_of(target * TILE + first, 8)
        scaled = []
        for axis in range(3):
            scaled.append(
                (geo[source, axis : axis + 1, :] - cols[axis, pl.ds(start, height), :])
                * (1.0 / cutoff_radius)
            )
        squared = scaled[0] * scaled[0] + scaled[1] * scaled[1] + scaled[2] * scaled[2]
        atom = lax.broadcasted_iota(jnp.int32, (height, LANES), 0) + first
        other = lane_atom + jnp.where(target == source, 0, TILE)
        use = (atom + target * TILE < count) & (atom != other)
        mask = jnp.where(use, geo[source, 3:4, :], 0.0)
        fade = jnp.maximum(1.0 - squared, 0.0)
        gaps = []
        bells = []
        for pair in range(BASIS // 2):
            center = jnp.where(upper, (2 * pair + 1) / (BASIS - 1), 2 * pair / (BASIS - 1))
            gap = squared - center
            gaps.append(gap)
            bells.append(jnp.exp(-basis_sharpness * (gap * gap)))
        sx, sy, sz = scaled
        angular = [
            None,
            root_three * sx,
            root_three * sy,
            root_three * sz,
            root_fifteen * sx * sy,
            root_fifteen * sy * sz,
            0.5 * root_five * (3.0 * sz * sz - squared),
            root_fifteen * sx * sz,
            0.5 * root_fifteen * (sx * sx - sy * sy),
        ]
        return scaled, mask, fade, gaps, bells, angular

    def forward(number, carry):
        target = pairs_ref[0, 0, number, 0]
        source = pairs_ref[0, 0, number, 1]
        right = hu_tab[source].astype(F32)
        for degree in range(3):
            for basis in range(BASIS):
                hw[number, degree, basis * TILE : (basis + 1) * TILE, :] = (
                    wrad_ref[basis, degree : degree + 1, :] * right
                ).astype(BF16)
        height = 16
        for first in range(0, TILE, height):
            scaled, mask, fade, gaps, bells, angular = scene(target, source, first, height)
            envelope = mask * (fade * fade * fade)
            for pair in range(BASIS // 2):
                radial = envelope * bells[pair]
                for order in range(ORDERS):
                    value = radial if order == 0 else angular[order] * radial
                    gb[
                        number,
                        order * TILE + first : order * TILE + first + height,
                        pair * LANES : (pair + 1) * LANES,
                    ] = value.astype(BF16)
        start = pl.multiple_of(target * TILE, TILE)
        for degree, (low, high) in enumerate(degree_limits):
            part = nn(gb[number, low * TILE : high * TILE, :], hw[number, degree])
            for order in range(low, high):
                sums[order, pl.ds(start, TILE), :] += part[
                    (order - low) * TILE : (order - low + 1) * TILE, :
                ]
        return carry

    lax.fori_loop(0, live, forward, 0)

    for degree, (low, high) in enumerate(degree_limits):
        for order in range(low, high):
            mixed[order] = nn((message_scale * sums[order]).astype(BF16), wmix_ref[degree])

    step = 16

    def squares(here):
        first_sq = sum(mixed[order, here, :] * mixed[order, here, :] for order in range(2, 4))
        first_sq = first_sq + mixed[1, here, :] * mixed[1, here, :]
        return first_sq

    def products(block, carry):
        here = pl.ds(pl.multiple_of(block * step, step), step)
        scalar = mixed[0, here, :]
        first_sq = squares(here)
        second_sq = mixed[4, here, :] * mixed[4, here, :]
        for order in range(5, 9):
            second_sq = second_sq + mixed[order, here, :] * mixed[order, here, :]
        prods[0, here, :] = scalar.astype(BF16)
        prods[1, here, :] = first_sq.astype(BF16)
        prods[2, here, :] = second_sq.astype(BF16)
        prods[3, here, :] = (scalar * first_sq).astype(BF16)
        return carry

    lax.fori_loop(0, rows // step, products, 0)
    message = nn(prods[0], wprod_ref[0])
    for part in range(1, 4):
        message = message + nn(prods[part], wprod_ref[part])
    sums[0] = message
    read = wread_ref[...]

    def gates(block, carry):
        here = pl.ds(pl.multiple_of(block * step, step), step)
        value = sums[0, here, :]
        gate = jax.nn.sigmoid(value)
        atom = lax.broadcasted_iota(jnp.int32, (step, channels), 0) + block * step
        weight = jnp.where(atom < count, read, 0.0)
        prods[0, here, :] = (weight * gate * (1.0 + value * (1.0 - gate))).astype(BF16)
        silu = value * gate * read
        top = silu.astype(BF16)
        prods[1, here, :] = top
        prods[2, here, :] = (silu - top.astype(F32)).astype(BF16)
        return carry

    lax.fori_loop(0, rows // step, gates, 0)
    ones = jnp.ones((8, channels), BF16)
    readout = (nt(ones, prods[1]) + nt(ones, prods[2]))[0:1, :]
    species = species_ref[0]
    reference_part = jnp.where(species == 0, eref_ref[0], eref_ref[1])
    atom_row = lax.broadcasted_iota(jnp.int32, (1, rows), 1)
    energy_ref[0] = jnp.where(atom_row < count, reference_part + readout, 0.0)
    for part in range(4):
        gprod[part] = nt(prods[0], wprod_ref[part])

    def unmix(block, carry):
        here = pl.ds(pl.multiple_of(block * step, step), step)
        scalar = mixed[0, here, :]
        last = gprod[3, here, :]
        gmix[0, here, :] = (gprod[0, here, :] + last * squares(here)).astype(BF16)
        factor = gprod[1, here, :] + last * scalar
        for order in range(1, 4):
            gmix[order, here, :] = (2.0 * mixed[order, here, :] * factor).astype(BF16)
        factor = gprod[2, here, :]
        for order in range(4, 9):
            gmix[order, here, :] = (2.0 * mixed[order, here, :] * factor).astype(BF16)
        return carry

    lax.fori_loop(0, rows // step, unmix, 0)
    for degree, (low, high) in enumerate(degree_limits):
        for order in range(low, high):
            back = (message_scale * nt(gmix[order], wmix_ref[degree])).astype(BF16)
            for tile in range(own_tiles):
                gat[tile, order * TILE : (order + 1) * TILE, :] = back[
                    tile * TILE : (tile + 1) * TILE, :
                ]

    def backward(number, carry):
        target = pairs_ref[0, 0, number, 0]
        source = pairs_ref[0, 0, number, 1]
        gather = jnp.zeros((TILE, channels), F32)
        for degree, (low, high) in enumerate(degree_limits):
            grads = gat[target, low * TILE : high * TILE, :]
            gg[low * TILE : high * TILE, :] = nt(grads, hw[number, degree])
            held = tn(gb[number, low * TILE : high * TILE, :], grads)
            for basis in range(BASIS):
                gather = gather + (
                    wrad_ref[basis, degree : degree + 1, :]
                    * held[basis * TILE : (basis + 1) * TILE, :]
                )
        ghu[source] += gather
        height = 8
        totals = [jnp.zeros((height, LANES), F32) for axis in range(3)]
        for first in range(0, TILE, height):
            scaled, mask, fade, gaps, bells, angular = scene(target, source, first, height)
            sx, sy, sz = scaled
            fade_sq = mask * (fade * fade)
            envelope = fade_sq * fade
            d_angular = [None] * ORDERS
            d_squared = None
            for pair in range(BASIS // 2):
                radial = envelope * bells[pair]
                d_radial = None
                for order in range(ORDERS):
                    grad = gg[
                        order * TILE + first : order * TILE + first + height,
                        pair * LANES : (pair + 1) * LANES,
                    ]
                    if order == 0:
                        d_radial = grad
                        continue
                    d_radial = d_radial + grad * angular[order]
                    term = grad * radial
                    d_angular[order] = term if pair == 0 else d_angular[order] + term
                term = (
                    d_radial
                    * bells[pair]
                    * (-3.0 - (2.0 * basis_sharpness) * (fade * gaps[pair]))
                )
                d_squared = term if pair == 0 else d_squared + term
            d_squared = d_squared * fade_sq - (0.5 * root_five) * d_angular[6]
            twice = 2.0 * d_squared
            d_x = (
                root_three * d_angular[1]
                + root_fifteen * (sy * d_angular[4] + sz * d_angular[7] + sx * d_angular[8])
                + sx * twice
            )
            d_y = (
                root_three * d_angular[2]
                + root_fifteen * (sx * d_angular[4] + sz * d_angular[5] - sy * d_angular[8])
                + sy * twice
            )
            d_z = (
                root_three * d_angular[3]
                + root_fifteen * (sy * d_angular[5] + sx * d_angular[7])
                + sz * (twice + (3.0 * root_five) * d_angular[6])
            )
            here = pl.ds(pl.multiple_of(target * TILE + first, 8), height)
            for axis, value in enumerate((d_x, d_y, d_z)):
                gpl[axis, here, :] += value
                totals[axis] = totals[axis] + value
        for axis in range(3):
            gpr[source, axis] += totals[axis]
        return carry

    lax.fori_loop(0, live, backward, 0)

    def folded(tile, axis):
        line = jnp.sum(gpr[tile, axis], axis=0, keepdims=True)
        return (line + pltpu.roll(line, TILE, 1)) * (1.0 / cutoff_radius)

    ones = jnp.ones((8, LANES), BF16)
    for axis in range(3):
        lefts = gpl[axis]
        top = lefts.astype(BF16)
        rest = (lefts - top.astype(F32)).astype(BF16)
        line = (nt(ones, top) + nt(ones, rest))[0:1, :] * (1.0 / cutoff_radius)
        rights = []
        for tile in range(0, own_tiles, 2):
            rights.append(jnp.where(upper, folded(tile + 1, axis), folded(tile, axis)))
        own_pos_ref[axis : axis + 1, :] = jnp.concatenate(rights, axis=1) - line
    own_pos_ref[3:8, :] = jnp.zeros((5, rows), F32)
    for tile in range(own_tiles):
        own_hu_ref[tile * TILE : (tile + 1) * TILE, :] = ghu[tile]
    for number in range(cells):
        msg_ref[number, 0:TILE, :] = ghu[own_tiles + number].astype(BF16)
        lines = [folded(own_tiles + number, axis) for axis in range(3)]
        tops = [line.astype(BF16).astype(F32) for line in lines]
        rests = [line - top for line, top in zip(lines, tops)]
        msg_ref[number, TILE : TILE + GEO, 0:LANES] = stack_rows(tops + rests, GEO, LANES).astype(BF16)
        msg_ref[number, TILE : TILE + GEO, LANES:channels] = jnp.zeros((GEO, channels - LANES), BF16)


def vmem():
    return pl.BlockSpec(memory_space=pltpu.VMEM)


def smem():
    return pl.BlockSpec(memory_space=pltpu.SMEM)


def body(
    nx,
    ny,
    positions,
    features,
    species,
    atom_count,
    quad_list,
    tile_pairs,
    w_up,
    w_radial,
    w_mix,
    w_prod,
    w_read,
    e_ref,
):
    rows = features.shape[2]
    channels = features.shape[3]
    cells = len(CELLS)
    own_tiles = rows // TILE
    tiles = own_tiles + cells
    max_pairs = tile_pairs.shape[2]
    block = TILE + GEO
    own_hu, ghosts = pl.pallas_call(
        functools.partial(halo_kernel, nx, ny),
        out_shape=(
            jax.ShapeDtypeStruct((rows, channels), BF16),
            jax.ShapeDtypeStruct((cells, block, channels), BF16),
        ),
        in_specs=[smem(), vmem(), vmem(), vmem(), vmem()],
        out_specs=(vmem(), vmem()),
        scratch_shapes=[
            pltpu.VMEM((4, block, channels), BF16),
            pltpu.SemaphoreType.DMA((cells,)),
            pltpu.SemaphoreType.DMA((cells,)),
        ],
        compiler_params=pltpu.CompilerParams(collective_id=0, has_side_effects=True),
        name="halo",
    )(atom_count, positions, features, quad_list, w_up)
    energies, messages, grad_hu, grad_pos = pl.pallas_call(
        core_kernel,
        out_shape=(
            jax.ShapeDtypeStruct((1, 1, rows), F32),
            jax.ShapeDtypeStruct((cells, block, channels), BF16),
            jax.ShapeDtypeStruct((rows, channels), F32),
            jax.ShapeDtypeStruct((8, rows), F32),
        ),
        in_specs=[smem(), smem(), smem()] + [vmem()] * 8,
        out_specs=(vmem(), vmem(), vmem(), vmem()),
        scratch_shapes=[
            pltpu.VMEM((tiles, TILE, channels), BF16),
            pltpu.VMEM((tiles, 8, LANES), F32),
            pltpu.VMEM((3, rows, LANES), F32),
            pltpu.VMEM((max_pairs, 3, BASIS * TILE, channels), BF16),
            pltpu.VMEM((max_pairs, ORDERS * TILE, BASIS * TILE), BF16),
            pltpu.VMEM((ORDERS, rows, channels), F32),
            pltpu.VMEM((ORDERS, rows, channels), F32),
            pltpu.VMEM((4, rows, channels), BF16),
            pltpu.VMEM((4, rows, channels), F32),
            pltpu.VMEM((ORDERS, rows, channels), BF16),
            pltpu.VMEM((own_tiles, ORDERS * TILE, channels), BF16),
            pltpu.VMEM((ORDERS * TILE, BASIS * TILE), F32),
            pltpu.VMEM((tiles, TILE, channels), F32),
            pltpu.VMEM((tiles, 3, 8, LANES), F32),
            pltpu.VMEM((3, rows, LANES), F32),
        ],
        compiler_params=pltpu.CompilerParams(vmem_limit_bytes=56 * 1024 * 1024),
        name="core",
    )(
        tile_pairs,
        atom_count,
        e_ref,
        positions,
        species,
        own_hu,
        ghosts,
        w_radial,
        w_mix,
        w_prod,
        w_read.reshape(1, channels),
    )
    forces, feature_grad = pl.pallas_call(
        functools.partial(return_kernel, nx, ny),
        out_shape=(
            jax.ShapeDtypeStruct((3, 1, 1, rows), F32),
            jax.ShapeDtypeStruct((1, 1, rows, channels), F32),
        ),
        in_specs=[pl.BlockSpec(memory_space=pl.ANY)] + [vmem()] * 4,
        out_specs=(vmem(), vmem()),
        scratch_shapes=[
            pltpu.VMEM((cells, block, channels), BF16),
            pltpu.VMEM((rows, channels), F32),
            pltpu.SemaphoreType.DMA((cells,)),
            pltpu.SemaphoreType.DMA((cells,)),
        ],
        compiler_params=pltpu.CompilerParams(collective_id=1, has_side_effects=True),
        name="giveback",
    )(messages, grad_hu, grad_pos, quad_list, w_up)
    return (energies, forces, feature_grad)


def solution(mesh):
    placed = (
        P(None, "gx", "gy", None),
        P("gx", "gy", None, None),
        P("gx", "gy", None),
        P("gx", "gy"),
        P("gx", "gy", None, None, None),
        P("gx", "gy", None, None),
        P(),
        P(),
        P(),
        P(),
        P(),
        P(),
    )
    return jax.shard_map(
        functools.partial(body, mesh.shape["gx"], mesh.shape["gy"]),
        mesh=mesh,
        in_specs=placed,
        out_specs=(P("gx", "gy", None), P(None, "gx", "gy", None), P("gx", "gy", None, None)),
        check_vma=False,
    )
```

```python
import functools

import jax
import jax.numpy as jnp
from jax import lax
from jax.experimental import pallas as pl
from jax.experimental.pallas import tpu as pltpu
from jax.sharding import PartitionSpec as P

BASIS = 8
TILE = 64
LANES = 128
GEO = 16
EXTRA = 8

cutoff_radius = 5.0
domain_width = 10.0
basis_sharpness = 10.0
message_scale = 0.25
degree_limits = ((0, 1), (1, 4), (4, 9))
ORDERS = 9
MESH = pl.DeviceIdType.MESH
F32 = jnp.float32
BF16 = jnp.bfloat16
root_three = 3.0**0.5
root_five = 5.0**0.5
root_fifteen = 15.0**0.5


def border_cells():
    return [(r, c) for r in range(4) for c in range(4) if r in (0, 3) or c in (0, 3)]


def cell_anchor(place):
    if place == 0:
        return (-1, 1)
    if place == 3:
        return (1, 0)
    return (0, place - 1)


def cell_table():
    listing = []
    for row, col in border_cells():
        dr, qx = cell_anchor(row)
        dc, qy = cell_anchor(col)
        listing.append((dr, dc, qx, qy))
    return listing


CELLS = cell_table()


def nn(left, right):
    return lax.dot_general(left, right, (((1,), (0,)), ((), ())), preferred_element_type=F32)


def nt(left, right):
    return lax.dot_general(left, right, (((1,), (1,)), ((), ())), preferred_element_type=F32)


def tn(left, right):
    return lax.dot_general(left, right, (((0,), (0,)), ((), ())), preferred_element_type=F32)


def three_parts(row):
    high = row.astype(BF16).astype(F32)
    rest = row - high
    middle = rest.astype(BF16).astype(F32)
    return high, middle, rest - middle


def stack_rows(rows, count, width):
    index = lax.broadcasted_iota(jnp.int32, (count, width), 0)
    out = jnp.zeros((count, width), F32)
    for number, row in enumerate(rows):
        out = jnp.where(index == number, row, out)
    return out


def position_parts(pos_ref):
    rows = []
    for axis in range(3):
        rows.extend(three_parts(pos_ref[axis, 0]))
    return stack_rows(rows, GEO, pos_ref.shape[3]).astype(BF16)


def neighbour(nx, ny, dx, dy):
    return (
        lax.rem(lax.axis_index("gx") + dx + nx, nx),
        lax.rem(lax.axis_index("gy") + dy + ny, ny),
    )


SIDES = ((1, 0), (-1, 0), (0, 1), (0, -1))
FACES = ((2, 1, 0), (3, 2, 0), (0, 9, 1), (1, 10, 1), (1, 4, 2), (3, 6, 2), (0, 5, 3), (2, 7, 3))
CORNERS = ((2, 0, 2), (1, 3, 3), (9, 11, 3), (10, 8, 2))


def side_of(nx, ny, side):
    return neighbour(nx, ny, *SIDES[side])


def greet(nx, ny):
    barrier = pltpu.get_barrier_semaphore()
    for side in range(4):
        pl.semaphore_signal(barrier, inc=1, device_id=side_of(nx, ny, side), device_id_type=MESH)
    return barrier


def halo_kernel(
    nx, ny, count_ref, pos_ref, feat_ref, quad_ref, wup_ref, hu_ref, cells_ref, outbox, send_sem, recv_sem
):
    barrier = greet(nx, ny)
    rows = feat_ref.shape[2]
    channels = feat_ref.shape[3]
    hu = nn(feat_ref[0, 0], wup_ref[...]).astype(BF16)
    hu_ref[...] = hu
    parts = position_parts(pos_ref)
    count = count_ref[0, 0]
    index = lax.broadcasted_iota(jnp.int32, (rows, TILE), 0)
    geo_row = lax.broadcasted_iota(jnp.int32, (GEO, LANES), 0)
    for qx in range(2):
        for qy in range(2):
            slot = quad_ref[0, 0, qx, pl.ds(qy, 1), :]
            hot = (index == slot).astype(F32).astype(BF16)
            quad = 2 * qx + qy
            outbox[quad, 0:TILE, :] = tn(hot, hu).astype(BF16)
            valid = jnp.where((slot >= 0) & (slot < count), 1.0, 0.0)
            geometry = nn(parts, jnp.concatenate([hot, hot], axis=1))
            both = jnp.concatenate([valid, valid], axis=1)
            geometry = jnp.where(geo_row == 9, both, geometry)
            wide = jnp.concatenate([geometry[0:EXTRA, :], geometry[EXTRA:GEO, :]], axis=1)
            outbox[quad, TILE : TILE + EXTRA, :] = wide.astype(BF16)
    pl.semaphore_wait(barrier, 4)

    def send(source, number, side):
        return pltpu.make_async_remote_copy(
            src_ref=source,
            dst_ref=cells_ref.at[number],
            send_sem=send_sem.at[number],
            recv_sem=recv_sem.at[number],
            device_id=side_of(nx, ny, side),
            device_id_type=MESH,
        )

    copies = {}
    for quad, number, side in FACES:
        copies[number] = send(outbox.at[quad], number, side)
        copies[number].start()
    for source, number, side in CORNERS:
        copies[source].wait_recv()
        copies[number] = send(cells_ref.at[source], number, side)
        copies[number].start()
    passed = [source for source, number, side in CORNERS]
    for number, copy in copies.items():
        if number not in passed:
            copy.wait_recv()
    for copy in copies.values():
        copy.wait_send()


def return_kernel(
    nx, ny, msg_ref, own_hu_ref, own_pos_ref, quad_ref, total_ref, shift_ref, inbox, joint, total, send_sem, recv_sem
):
    barrier = greet(nx, ny)
    rows = own_hu_ref.shape[0]
    pl.semaphore_wait(barrier, 4)

    def send(source, number, side):
        return pltpu.make_async_remote_copy(
            src_ref=source,
            dst_ref=inbox.at[number],
            send_sem=send_sem.at[number],
            recv_sem=recv_sem.at[number],
            device_id=side_of(nx, ny, side ^ 1),
            device_id_type=MESH,
        )

    copies = {}
    for face, number, side in CORNERS:
        copies[number] = send(msg_ref.at[number], number, side)
        copies[number].start()
    for quad, number, side in FACES[4:]:
        copies[number] = send(msg_ref.at[number], number, side)
        copies[number].start()
    sides = {number: (quad, side) for quad, number, side in FACES}
    for place, (face, number, side) in enumerate(CORNERS):
        copies[number].wait_recv()
        joint[place] = (msg_ref[face].astype(F32) + inbox[number].astype(F32)).astype(BF16)
        copies[face] = send(joint.at[place], face, sides[face][1])
        copies[face].start()
    index = lax.broadcasted_iota(jnp.int32, (rows, TILE), 0)
    hots = []
    for qx in range(2):
        for qy in range(2):
            hots.append((index == quad_ref[0, 0, qx, pl.ds(qy, 1), :]).astype(F32).astype(BF16))
    total[...] = own_hu_ref[...]
    shifts = jnp.zeros((EXTRA, rows), F32)
    for quad, number, side in FACES[4:] + FACES[:4]:
        copies[number].wait_recv()
        total[...] += nn(hots[quad], inbox[number, 0:TILE, :])
        shifts = shifts + nt(inbox[number, TILE : TILE + EXTRA, 0:TILE], hots[quad])
    total_ref[...] = total[...].astype(BF16)
    shift_ref[...] = own_pos_ref[...] + shifts
    for copy in copies.values():
        copy.wait_send()


def finish_kernel(total_ref, shift_ref, wup_ref, force_ref, grad_ref):
    for axis in range(3):
        force_ref[axis, 0] = -(shift_ref[axis : axis + 1, :] + shift_ref[3 + axis : 4 + axis, :])
    grad_ref[0, 0] = nt(total_ref[...], wup_ref[...])


def core_kernel(
    pairs_ref,
    count_ref,
    eref_ref,
    pos_ref,
    species_ref,
    hu_ref,
    cells_ref,
    wrad_ref,
    wmix_ref,
    wprod_ref,
    wread_ref,
    energy_ref,
    msg_ref,
    own_hu_ref,
    own_pos_ref,
    hu_tab,
    geo,
    cols,
    hw,
    gb,
    sums,
    mixed,
    prods,
    gprod,
    gmix,
    gat,
    gg,
    ghu,
    gpr,
    gpl,
):
    rows, channels = hu_ref.shape
    own_tiles = rows // TILE
    cells = cells_ref.shape[0]
    tiles = own_tiles + cells
    max_pairs = pairs_ref.shape[3]
    count = count_ref[0, 0]
    live = jnp.int32(0)
    for number in range(max_pairs):
        live = live + jnp.where(pairs_ref[0, 0, 0, number] >= 0, 1, 0)

    parts = position_parts(pos_ref)
    lane = lax.broadcasted_iota(jnp.int32, (1, LANES), 1)
    lane_atom = lax.rem(lane, TILE)
    upper = lane >= TILE
    geo_row = lax.broadcasted_iota(jnp.int32, (8, LANES), 0)

    def set_geometry(tile, raw, valid, shift):
        coords = []
        for axis in range(3):
            first = 3 * axis
            whole = (
                raw[first : first + 1, :] + raw[first + 1 : first + 2, :]
            ) + raw[first + 2 : first + 3, :]
            coords.append(whole + shift[axis])
        geo[tile] = stack_rows(coords + [valid], 8, LANES)

    square = lax.broadcasted_iota(jnp.int32, (rows, LANES), 0)
    for tile in range(own_tiles):
        hu_tab[tile] = hu_ref[tile * TILE : (tile + 1) * TILE, :]
        slot = lane_atom + tile * TILE
        hot = (square == slot).astype(F32).astype(BF16)
        set_geometry(tile, nn(parts, hot), jnp.where(slot < count, 1.0, 0.0), (0.0, 0.0, 0.0))
    for number, (dr, dc, qx, qy) in enumerate(CELLS):
        hu_tab[own_tiles + number] = cells_ref[number, 0:TILE, :]
        wide = cells_ref[number, TILE : TILE + EXTRA, :].astype(F32)
        raw = jnp.concatenate([wide[:, 0:LANES], wide[:, LANES : 2 * LANES]], axis=0)
        set_geometry(
            own_tiles + number, raw, raw[9:10, :], (dr * domain_width, dc * domain_width, 0.0)
        )
    eye = (
        lax.broadcasted_iota(jnp.int32, (rows, rows), 0)
        == lax.broadcasted_iota(jnp.int32, (rows, rows), 1)
    ).astype(F32).astype(BF16)
    columns = nt(eye, parts)
    for axis in range(3):
        first = 3 * axis
        whole = (columns[:, first : first + 1] + columns[:, first + 1 : first + 2]) + columns[
            :, first + 2 : first + 3
        ]
        cols[axis] = jnp.broadcast_to(whole, (rows, LANES))
    sums[...] = jnp.zeros_like(sums)
    ghu[...] = jnp.zeros_like(ghu)
    gpr[...] = jnp.zeros_like(gpr)
    gpl[...] = jnp.zeros_like(gpl)

    def scene(target, source, first, height):
        start = pl.multiple_of(target * TILE + first, 8)
        scaled = []
        for axis in range(3):
            scaled.append(
                (geo[source, axis : axis + 1, :] - cols[axis, pl.ds(start, height), :])
                * (1.0 / cutoff_radius)
            )
        squared = scaled[0] * scaled[0] + scaled[1] * scaled[1] + scaled[2] * scaled[2]
        atom = lax.broadcasted_iota(jnp.int32, (height, LANES), 0) + first
        other = lane_atom + jnp.where(target == source, 0, TILE)
        use = (atom + target * TILE < count) & (atom != other)
        mask = jnp.where(use, geo[source, 3:4, :], 0.0)
        fade = jnp.maximum(1.0 - squared, 0.0)
        gaps = []
        bells = []
        for pair in range(BASIS // 2):
            center = jnp.where(upper, (2 * pair + 1) / (BASIS - 1), 2 * pair / (BASIS - 1))
            gap = squared - center
            gaps.append(gap)
            bells.append(jnp.exp(-basis_sharpness * (gap * gap)))
        sx, sy, sz = scaled
        angular = [
            None,
            root_three * sx,
            root_three * sy,
            root_three * sz,
            root_fifteen * sx * sy,
            root_fifteen * sy * sz,
            0.5 * root_five * (3.0 * sz * sz - squared),
            root_fifteen * sx * sz,
            0.5 * root_fifteen * (sx * sx - sy * sy),
        ]
        return scaled, mask, fade, gaps, bells, angular

    def forward(number, carry):
        target = pairs_ref[0, 0, 0, number]
        source = pairs_ref[0, 0, 1, number]
        last, place = carry
        fresh = source != last
        place = jnp.where(fresh, place + 1, place)

        @pl.when(fresh)
        def _():
            right = hu_tab[source].astype(F32)
            for degree in range(3):
                for basis in range(BASIS):
                    hw[place, degree, basis * TILE : (basis + 1) * TILE, :] = (
                        wrad_ref[degree, basis : basis + 1, :] * right
                    ).astype(BF16)

        height = 16
        for first in range(0, TILE, height):
            scaled, mask, fade, gaps, bells, angular = scene(target, source, first, height)
            envelope = mask * (fade * fade * fade)
            for pair in range(BASIS // 2):
                radial = envelope * bells[pair]
                for order in range(ORDERS):
                    value = radial if order == 0 else angular[order] * radial
                    gb[
                        number,
                        order * TILE + first : order * TILE + first + height,
                        pair * LANES : (pair + 1) * LANES,
                    ] = value.astype(BF16)
        start = pl.multiple_of(target * TILE, TILE)
        for degree, (low, high) in enumerate(degree_limits):
            part = nn(gb[number, low * TILE : high * TILE, :], hw[place, degree])
            for order in range(low, high):
                sums[order, pl.ds(start, TILE), :] += part[
                    (order - low) * TILE : (order - low + 1) * TILE, :
                ]
        return source, place

    lax.fori_loop(0, live, forward, (jnp.int32(-1), jnp.int32(-1)))

    for degree, (low, high) in enumerate(degree_limits):
        for order in range(low, high):
            mixed[order] = nn((message_scale * sums[order]).astype(BF16), wmix_ref[degree])

    step = 16

    def squares(here):
        first_sq = sum(mixed[order, here, :] * mixed[order, here, :] for order in range(2, 4))
        first_sq = first_sq + mixed[1, here, :] * mixed[1, here, :]
        return first_sq

    def products(block, carry):
        here = pl.ds(pl.multiple_of(block * step, step), step)
        scalar = mixed[0, here, :]
        first_sq = squares(here)
        second_sq = mixed[4, here, :] * mixed[4, here, :]
        for order in range(5, 9):
            second_sq = second_sq + mixed[order, here, :] * mixed[order, here, :]
        prods[0, here, :] = scalar.astype(BF16)
        prods[1, here, :] = first_sq.astype(BF16)
        prods[2, here, :] = second_sq.astype(BF16)
        prods[3, here, :] = (scalar * first_sq).astype(BF16)
        return carry

    lax.fori_loop(0, rows // step, products, 0)
    message = nn(prods[0], wprod_ref[0])
    for part in range(1, 4):
        message = message + nn(prods[part], wprod_ref[part])
    sums[0] = message
    read = wread_ref[...]

    def gates(block, carry):
        here = pl.ds(pl.multiple_of(block * step, step), step)
        value = sums[0, here, :]
        gate = jax.nn.sigmoid(value)
        atom = lax.broadcasted_iota(jnp.int32, (step, channels), 0) + block * step
        weight = jnp.where(atom < count, read, 0.0)
        prods[0, here, :] = (weight * gate * (1.0 + value * (1.0 - gate))).astype(BF16)
        silu = value * gate * read
        top = silu.astype(BF16)
        prods[1, here, :] = top
        prods[2, here, :] = (silu - top.astype(F32)).astype(BF16)
        return carry

    lax.fori_loop(0, rows // step, gates, 0)
    ones = jnp.ones((8, channels), BF16)
    readout = (nt(ones, prods[1]) + nt(ones, prods[2]))[0:1, :]
    species = species_ref[0]
    reference_part = jnp.where(species == 0, eref_ref[0], eref_ref[1])
    atom_row = lax.broadcasted_iota(jnp.int32, (1, rows), 1)
    energy_ref[0] = jnp.where(atom_row < count, reference_part + readout, 0.0)
    for part in range(4):
        gprod[part] = nt(prods[0], wprod_ref[part])

    def unmix(block, carry):
        here = pl.ds(pl.multiple_of(block * step, step), step)
        scalar = mixed[0, here, :]
        last = gprod[3, here, :]
        gmix[0, here, :] = (gprod[0, here, :] + last * squares(here)).astype(BF16)
        factor = gprod[1, here, :] + last * scalar
        for order in range(1, 4):
            gmix[order, here, :] = (2.0 * mixed[order, here, :] * factor).astype(BF16)
        factor = gprod[2, here, :]
        for order in range(4, 9):
            gmix[order, here, :] = (2.0 * mixed[order, here, :] * factor).astype(BF16)
        return carry

    lax.fori_loop(0, rows // step, unmix, 0)
    for degree, (low, high) in enumerate(degree_limits):
        for order in range(low, high):
            back = (message_scale * nt(gmix[order], wmix_ref[degree])).astype(BF16)
            for tile in range(own_tiles):
                gat[tile, order * TILE : (order + 1) * TILE, :] = back[
                    tile * TILE : (tile + 1) * TILE, :
                ]

    def backward(number, carry):
        target = pairs_ref[0, 0, 0, number]
        source = pairs_ref[0, 0, 1, number]
        last, place = carry
        place = jnp.where(source != last, place + 1, place)
        gather = jnp.zeros((TILE, channels), F32)
        for degree, (low, high) in enumerate(degree_limits):
            grads = gat[target, low * TILE : high * TILE, :]
            gg[low * TILE : high * TILE, :] = nt(grads, hw[place, degree])
            held = tn(gb[number, low * TILE : high * TILE, :], grads)
            for basis in range(BASIS):
                gather = gather + (
                    wrad_ref[degree, basis : basis + 1, :]
                    * held[basis * TILE : (basis + 1) * TILE, :]
                )
        ghu[source] += gather
        height = 8
        totals = [jnp.zeros((height, LANES), F32) for axis in range(3)]
        for first in range(0, TILE, height):
            scaled, mask, fade, gaps, bells, angular = scene(target, source, first, height)
            sx, sy, sz = scaled
            fade_sq = mask * (fade * fade)
            envelope = fade_sq * fade
            d_angular = [None] * ORDERS
            d_squared = None
            for pair in range(BASIS // 2):
                radial = envelope * bells[pair]
                d_radial = None
                for order in range(ORDERS):
                    grad = gg[
                        order * TILE + first : order * TILE + first + height,
                        pair * LANES : (pair + 1) * LANES,
                    ]
                    if order == 0:
                        d_radial = grad
                        continue
                    d_radial = d_radial + grad * angular[order]
                    term = grad * radial
                    d_angular[order] = term if pair == 0 else d_angular[order] + term
                term = (
                    d_radial
                    * bells[pair]
                    * (-3.0 - (2.0 * basis_sharpness) * (fade * gaps[pair]))
                )
                d_squared = term if pair == 0 else d_squared + term
            d_squared = d_squared * fade_sq - (0.5 * root_five) * d_angular[6]
            twice = 2.0 * d_squared
            d_x = (
                root_three * d_angular[1]
                + root_fifteen * (sy * d_angular[4] + sz * d_angular[7] + sx * d_angular[8])
                + sx * twice
            )
            d_y = (
                root_three * d_angular[2]
                + root_fifteen * (sx * d_angular[4] + sz * d_angular[5] - sy * d_angular[8])
                + sy * twice
            )
            d_z = (
                root_three * d_angular[3]
                + root_fifteen * (sy * d_angular[5] + sx * d_angular[7])
                + sz * (twice + (3.0 * root_five) * d_angular[6])
            )
            here = pl.ds(pl.multiple_of(target * TILE + first, 8), height)
            for axis, value in enumerate((d_x, d_y, d_z)):
                gpl[axis, here, :] += value
                totals[axis] = totals[axis] + value
        for axis in range(3):
            gpr[source, axis] += totals[axis]
        return source, place

    lax.fori_loop(0, live, backward, (jnp.int32(-1), jnp.int32(-1)))

    def folded(tile, axis):
        line = jnp.sum(gpr[tile, axis], axis=0, keepdims=True)
        return (line + pltpu.roll(line, TILE, 1)) * (1.0 / cutoff_radius)

    ones = jnp.ones((8, LANES), BF16)
    for axis in range(3):
        lefts = gpl[axis]
        top = lefts.astype(BF16)
        rest = (lefts - top.astype(F32)).astype(BF16)
        line = (nt(ones, top) + nt(ones, rest))[0:1, :] * (1.0 / cutoff_radius)
        rights = []
        for tile in range(0, own_tiles, 2):
            rights.append(jnp.where(upper, folded(tile + 1, axis), folded(tile, axis)))
        own_pos_ref[axis : axis + 1, :] = jnp.concatenate(rights, axis=1) - line
    own_pos_ref[3:8, :] = jnp.zeros((5, rows), F32)
    for tile in range(own_tiles):
        own_hu_ref[tile * TILE : (tile + 1) * TILE, :] = ghu[tile]
    for number in range(cells):
        msg_ref[number, 0:TILE, :] = ghu[own_tiles + number].astype(BF16)
        lines = [folded(own_tiles + number, axis) for axis in range(3)]
        tops = [line.astype(BF16).astype(F32) for line in lines]
        rests = [line - top for line, top in zip(lines, tops)]
        packed = stack_rows(tops + rests, EXTRA, LANES)
        fill = jnp.zeros((EXTRA, channels - LANES), F32)
        msg_ref[number, TILE : TILE + EXTRA, :] = jnp.concatenate([packed, fill], axis=1).astype(BF16)


def vmem():
    return pl.BlockSpec(memory_space=pltpu.VMEM)


def smem():
    return pl.BlockSpec(memory_space=pltpu.SMEM)


def body(
    nx,
    ny,
    positions,
    features,
    species,
    atom_count,
    quad_list,
    tile_pairs,
    w_up,
    w_radial,
    w_mix,
    w_prod,
    w_read,
    e_ref,
):
    rows = features.shape[2]
    channels = features.shape[3]
    cells = len(CELLS)
    own_tiles = rows // TILE
    tiles = own_tiles + cells
    max_pairs = tile_pairs.shape[2]
    block = TILE + EXTRA
    own_hu, ghosts = pl.pallas_call(
        functools.partial(halo_kernel, nx, ny),
        out_shape=(
            jax.ShapeDtypeStruct((rows, channels), BF16),
            jax.ShapeDtypeStruct((cells, block, channels), BF16),
        ),
        in_specs=[smem(), vmem(), vmem(), vmem(), vmem()],
        out_specs=(vmem(), vmem()),
        scratch_shapes=[
            pltpu.VMEM((4, block, channels), BF16),
            pltpu.SemaphoreType.DMA((cells,)),
            pltpu.SemaphoreType.DMA((cells,)),
        ],
        compiler_params=pltpu.CompilerParams(
            collective_id=0, has_side_effects=True, vmem_limit_bytes=6 * 1024 * 1024
        ),
        name="halo",
    )(atom_count, positions, features, quad_list, w_up)
    energies, messages, grad_hu, grad_pos = pl.pallas_call(
        core_kernel,
        out_shape=(
            jax.ShapeDtypeStruct((1, 1, rows), F32),
            jax.ShapeDtypeStruct((cells, block, channels), BF16),
            jax.ShapeDtypeStruct((rows, channels), F32),
            jax.ShapeDtypeStruct((8, rows), F32),
        ),
        in_specs=[smem(), smem(), smem()] + [vmem()] * 8,
        out_specs=(vmem(), vmem(), vmem(), vmem()),
        scratch_shapes=[
            pltpu.VMEM((tiles, TILE, channels), BF16),
            pltpu.VMEM((tiles, 8, LANES), F32),
            pltpu.VMEM((3, rows, LANES), F32),
            pltpu.VMEM((max_pairs, 3, BASIS * TILE, channels), BF16),
            pltpu.VMEM((max_pairs, ORDERS * TILE, BASIS * TILE), BF16),
            pltpu.VMEM((ORDERS, rows, channels), F32),
            pltpu.VMEM((ORDERS, rows, channels), F32),
            pltpu.VMEM((4, rows, channels), BF16),
            pltpu.VMEM((4, rows, channels), F32),
            pltpu.VMEM((ORDERS, rows, channels), BF16),
            pltpu.VMEM((own_tiles, ORDERS * TILE, channels), BF16),
            pltpu.VMEM((ORDERS * TILE, BASIS * TILE), F32),
            pltpu.VMEM((tiles, TILE, channels), F32),
            pltpu.VMEM((tiles, 3, 8, LANES), F32),
            pltpu.VMEM((3, rows, LANES), F32),
        ],
        compiler_params=pltpu.CompilerParams(vmem_limit_bytes=40 * 1024 * 1024),
        name="core",
    )(
        jnp.swapaxes(tile_pairs, 2, 3),
        atom_count,
        e_ref,
        positions,
        species,
        own_hu,
        ghosts,
        jnp.swapaxes(w_radial, 0, 1),
        w_mix,
        w_prod,
        w_read.reshape(1, channels),
    )
    total, shifts = pl.pallas_call(
        functools.partial(return_kernel, nx, ny),
        out_shape=(
            jax.ShapeDtypeStruct((rows, channels), BF16),
            jax.ShapeDtypeStruct((8, rows), F32),
        ),
        in_specs=[vmem()] * 4,
        out_specs=(vmem(), vmem()),
        scratch_shapes=[
            pltpu.VMEM((cells, block, channels), BF16),
            pltpu.VMEM((4, block, channels), BF16),
            pltpu.VMEM((rows, channels), F32),
            pltpu.SemaphoreType.DMA((cells,)),
            pltpu.SemaphoreType.DMA((cells,)),
        ],
        compiler_params=pltpu.CompilerParams(
            collective_id=1, has_side_effects=True, vmem_limit_bytes=8 * 1024 * 1024
        ),
        name="giveback",
    )(messages, grad_hu, grad_pos, quad_list)
    forces, feature_grad = pl.pallas_call(
        finish_kernel,
        out_shape=(
            jax.ShapeDtypeStruct((3, 1, 1, rows), F32),
            jax.ShapeDtypeStruct((1, 1, rows, channels), F32),
        ),
        in_specs=[vmem()] * 3,
        out_specs=(vmem(), vmem()),
        compiler_params=pltpu.CompilerParams(vmem_limit_bytes=4 * 1024 * 1024),
        name="finish",
    )(total, shifts, w_up)
    return (energies, forces, feature_grad)


def solution(mesh):
    placed = (
        P(None, "gx", "gy", None),
        P("gx", "gy", None, None),
        P("gx", "gy", None),
        P("gx", "gy"),
        P("gx", "gy", None, None, None),
        P("gx", "gy", None, None),
        P(),
        P(),
        P(),
        P(),
        P(),
        P(),
    )
    return jax.shard_map(
        functools.partial(body, mesh.shape["gx"], mesh.shape["gy"]),
        mesh=mesh,
        in_specs=placed,
        out_specs=(P("gx", "gy", None), P(None, "gx", "gy", None), P("gx", "gy", None, None)),
        check_vma=False,
    )
```

```python
import functools

import jax
import jax.numpy as jnp
from jax import lax
from jax.experimental import pallas as pl
from jax.experimental.pallas import tpu as pltpu
from jax.sharding import PartitionSpec as P

BASIS = 8
TILE = 64
LANES = 128
GEO = 16
EXTRA = 8

cutoff_radius = 5.0
domain_width = 10.0
basis_sharpness = 10.0
message_scale = 0.25
degree_limits = ((0, 1), (1, 4), (4, 9))
ORDERS = 9
MESH = pl.DeviceIdType.MESH
F32 = jnp.float32
BF16 = jnp.bfloat16
root_three = 3.0**0.5
root_five = 5.0**0.5
root_fifteen = 15.0**0.5


def border_cells():
    return [(r, c) for r in range(4) for c in range(4) if r in (0, 3) or c in (0, 3)]


def cell_anchor(place):
    if place == 0:
        return (-1, 1)
    if place == 3:
        return (1, 0)
    return (0, place - 1)


def cell_table():
    listing = []
    for row, col in border_cells():
        dr, qx = cell_anchor(row)
        dc, qy = cell_anchor(col)
        listing.append((dr, dc, qx, qy))
    return listing


CELLS = cell_table()


def nn(left, right):
    return lax.dot_general(left, right, (((1,), (0,)), ((), ())), preferred_element_type=F32)


def nt(left, right):
    return lax.dot_general(left, right, (((1,), (1,)), ((), ())), preferred_element_type=F32)


def tn(left, right):
    return lax.dot_general(left, right, (((0,), (0,)), ((), ())), preferred_element_type=F32)


def three_parts(row):
    high = row.astype(BF16).astype(F32)
    rest = row - high
    middle = rest.astype(BF16).astype(F32)
    return high, middle, rest - middle


def stack_rows(rows, count, width):
    index = lax.broadcasted_iota(jnp.int32, (count, width), 0)
    out = jnp.zeros((count, width), F32)
    for number, row in enumerate(rows):
        out = jnp.where(index == number, row, out)
    return out


def position_parts(pos_ref):
    rows = []
    for axis in range(3):
        rows.extend(three_parts(pos_ref[axis, 0]))
    return stack_rows(rows, GEO, pos_ref.shape[3]).astype(BF16)


def geometry_rows(raw, valid, shift):
    coords = []
    for axis in range(3):
        first = 3 * axis
        whole = (raw[first : first + 1, :] + raw[first + 1 : first + 2, :]) + raw[
            first + 2 : first + 3, :
        ]
        coords.append(whole + shift[axis])
    return stack_rows(coords + [valid], 8, LANES)


def neighbour(nx, ny, dx, dy):
    return (
        lax.rem(lax.axis_index("gx") + dx + nx, nx),
        lax.rem(lax.axis_index("gy") + dy + ny, ny),
    )


SIDES = ((1, 0), (-1, 0), (0, 1), (0, -1))
FACES = ((2, 1, 0), (3, 2, 0), (0, 9, 1), (1, 10, 1), (1, 4, 2), (3, 6, 2), (0, 5, 3), (2, 7, 3))
CORNERS = ((2, 0, 2), (1, 3, 3), (9, 11, 3), (10, 8, 2))


def side_of(nx, ny, side):
    return neighbour(nx, ny, *SIDES[side])


def greet(nx, ny):
    barrier = pltpu.get_barrier_semaphore()
    for side in range(4):
        pl.semaphore_signal(barrier, inc=1, device_id=side_of(nx, ny, side), device_id_type=MESH)
    return barrier


def halo_kernel(
    nx,
    ny,
    count_ref,
    pos_hbm,
    feat_hbm,
    quad_hbm,
    wup_hbm,
    cells_ref,
    geo_ref,
    cols_ref,
    outbox,
    pos_ref,
    feat_ref,
    quad_ref,
    wup_ref,
    fetch_sem,
    send_sem,
    recv_sem,
):
    pulls = [
        pltpu.make_async_copy(source, target, fetch_sem.at[number])
        for number, (source, target) in enumerate(
            ((feat_hbm, feat_ref), (wup_hbm, wup_ref), (pos_hbm, pos_ref), (quad_hbm, quad_ref))
        )
    ]
    for pull in pulls:
        pull.start()
    barrier = greet(nx, ny)
    rows = feat_ref.shape[2]
    channels = feat_ref.shape[3]
    own_tiles = rows // TILE
    for pull in pulls:
        pull.wait()
    hu = nn(feat_ref[0, 0], wup_ref[...]).astype(BF16)
    for tile in range(own_tiles):
        cells_ref[tile, 0:TILE, :] = hu[tile * TILE : (tile + 1) * TILE, :]
    parts = position_parts(pos_ref)
    count = count_ref[0, 0]
    index = lax.broadcasted_iota(jnp.int32, (rows, TILE), 0)
    geo_row = lax.broadcasted_iota(jnp.int32, (GEO, LANES), 0)
    for qx in range(2):
        for qy in range(2):
            slot = quad_ref[0, 0, qx, pl.ds(qy, 1), :]
            hot = (index == slot).astype(F32).astype(BF16)
            quad = 2 * qx + qy
            outbox[quad, 0:TILE, :] = tn(hot, hu).astype(BF16)
            valid = jnp.where((slot >= 0) & (slot < count), 1.0, 0.0)
            geometry = nn(parts, jnp.concatenate([hot, hot], axis=1))
            both = jnp.concatenate([valid, valid], axis=1)
            geometry = jnp.where(geo_row == 9, both, geometry)
            wide = jnp.concatenate([geometry[0:EXTRA, :], geometry[EXTRA:GEO, :]], axis=1)
            outbox[quad, TILE : TILE + EXTRA, :] = wide.astype(BF16)
    pl.semaphore_wait(barrier, 4)

    def send(source, number, side):
        return pltpu.make_async_remote_copy(
            src_ref=source,
            dst_ref=cells_ref.at[own_tiles + number],
            send_sem=send_sem.at[number],
            recv_sem=recv_sem.at[number],
            device_id=side_of(nx, ny, side),
            device_id_type=MESH,
        )

    copies = {}
    for quad, number, side in FACES:
        copies[number] = send(outbox.at[quad], number, side)
        copies[number].start()
    lane_atom = lax.rem(lax.broadcasted_iota(jnp.int32, (1, LANES), 1), TILE)
    square = lax.broadcasted_iota(jnp.int32, (rows, LANES), 0)
    for tile in range(own_tiles):
        slot = lane_atom + tile * TILE
        hot = (square == slot).astype(F32).astype(BF16)
        geo_ref[tile] = geometry_rows(
            nn(parts, hot), jnp.where(slot < count, 1.0, 0.0), (0.0, 0.0, 0.0)
        )
    eye = (
        lax.broadcasted_iota(jnp.int32, (rows, rows), 0)
        == lax.broadcasted_iota(jnp.int32, (rows, rows), 1)
    )
    columns = nt(eye.astype(F32).astype(BF16), parts)
    for axis in range(3):
        first = 3 * axis
        whole = (columns[:, first : first + 1] + columns[:, first + 1 : first + 2]) + columns[
            :, first + 2 : first + 3
        ]
        cols_ref[axis] = jnp.broadcast_to(whole, (rows, LANES))
    for source, number, side in CORNERS:
        copies[source].wait_recv()
        copies[number] = send(cells_ref.at[own_tiles + source], number, side)
        copies[number].start()
    passed = [source for source, number, side in CORNERS]
    for number, copy in copies.items():
        if number not in passed:
            copy.wait_recv()
    for copy in copies.values():
        copy.wait_send()


def return_kernel(
    nx, ny, msg_ref, own_hu_ref, own_pos_ref, quad_ref, total_ref, shift_ref, inbox, joint, total, send_sem, recv_sem
):
    barrier = greet(nx, ny)
    rows = own_hu_ref.shape[0]
    pl.semaphore_wait(barrier, 4)

    def send(source, number, side):
        return pltpu.make_async_remote_copy(
            src_ref=source,
            dst_ref=inbox.at[number],
            send_sem=send_sem.at[number],
            recv_sem=recv_sem.at[number],
            device_id=side_of(nx, ny, side ^ 1),
            device_id_type=MESH,
        )

    copies = {}
    for face, number, side in CORNERS:
        copies[number] = send(msg_ref.at[number], number, side)
        copies[number].start()
    for quad, number, side in FACES[4:]:
        copies[number] = send(msg_ref.at[number], number, side)
        copies[number].start()
    sides = {number: (quad, side) for quad, number, side in FACES}
    for place, (face, number, side) in enumerate(CORNERS):
        copies[number].wait_recv()
        joint[place] = (msg_ref[face].astype(F32) + inbox[number].astype(F32)).astype(BF16)
        copies[face] = send(joint.at[place], face, sides[face][1])
        copies[face].start()
    index = lax.broadcasted_iota(jnp.int32, (rows, TILE), 0)
    hots = []
    for qx in range(2):
        for qy in range(2):
            hots.append((index == quad_ref[0, 0, qx, pl.ds(qy, 1), :]).astype(F32).astype(BF16))
    total[...] = own_hu_ref[...]
    shifts = jnp.zeros((EXTRA, rows), F32)
    for quad, number, side in FACES[4:] + FACES[:4]:
        copies[number].wait_recv()
        total[...] += nn(hots[quad], inbox[number, 0:TILE, :])
        shifts = shifts + nt(inbox[number, TILE : TILE + EXTRA, 0:TILE], hots[quad])
    total_ref[...] = total[...].astype(BF16)
    shift_ref[...] = own_pos_ref[...] + shifts
    for copy in copies.values():
        copy.wait_send()


def finish_kernel(total_ref, shift_ref, wup_ref, force_ref, grad_ref):
    for axis in range(3):
        force_ref[axis, 0] = -(shift_ref[axis : axis + 1, :] + shift_ref[3 + axis : 4 + axis, :])
    grad_ref[0, 0] = nt(total_ref[...], wup_ref[...])


def core_kernel(
    count_ref,
    eref_ref,
    pairs_hbm,
    wmix_hbm,
    wprod_hbm,
    species_ref,
    hu_tab,
    geo_ref,
    cols,
    wrad_ref,
    wread_ref,
    energy_ref,
    msg_ref,
    own_hu_ref,
    own_pos_ref,
    pairs_ref,
    wmix_ref,
    wprod_ref,
    fetch_sem,
    geo,
    hw,
    gb,
    sums,
    mixed,
    prods,
    gprod,
    gmix,
    gat,
    gg,
    ghu,
    gpr,
    gpl,
):
    pulls = [
        pltpu.make_async_copy(source, target, fetch_sem.at[number])
        for number, (source, target) in enumerate(
            ((pairs_hbm, pairs_ref), (wmix_hbm, wmix_ref), (wprod_hbm, wprod_ref))
        )
    ]
    for pull in pulls:
        pull.start()
    rows, channels = own_hu_ref.shape
    own_tiles = rows // TILE
    cells = msg_ref.shape[0]
    max_pairs = pairs_ref.shape[3]
    count = count_ref[0, 0]
    lane = lax.broadcasted_iota(jnp.int32, (1, LANES), 1)
    lane_atom = lax.rem(lane, TILE)
    upper = lane >= TILE
    for tile in range(own_tiles):
        geo[tile] = geo_ref[tile]
    for number, (dr, dc, qx, qy) in enumerate(CELLS):
        wide = hu_tab[own_tiles + number, TILE : TILE + EXTRA, :].astype(F32)
        raw = jnp.concatenate([wide[:, 0:LANES], wide[:, LANES : 2 * LANES]], axis=0)
        geo[own_tiles + number] = geometry_rows(
            raw, raw[9:10, :], (dr * domain_width, dc * domain_width, 0.0)
        )
    sums[...] = jnp.zeros_like(sums)
    ghu[...] = jnp.zeros_like(ghu)
    gpr[...] = jnp.zeros_like(gpr)
    gpl[...] = jnp.zeros_like(gpl)

    pulls[0].wait()
    live = jnp.int32(0)
    for number in range(max_pairs):
        live = live + jnp.where(pairs_ref[0, 0, 0, number] >= 0, 1, 0)

    def scene(target, source, first, height):
        start = pl.multiple_of(target * TILE + first, 8)
        scaled = []
        for axis in range(3):
            scaled.append(
                (geo[source, axis : axis + 1, :] - cols[axis, pl.ds(start, height), :])
                * (1.0 / cutoff_radius)
            )
        squared = scaled[0] * scaled[0] + scaled[1] * scaled[1] + scaled[2] * scaled[2]
        atom = lax.broadcasted_iota(jnp.int32, (height, LANES), 0) + first
        other = lane_atom + jnp.where(target == source, 0, TILE)
        use = (atom + target * TILE < count) & (atom != other)
        mask = jnp.where(use, geo[source, 3:4, :], 0.0)
        fade = jnp.maximum(1.0 - squared, 0.0)
        gaps = []
        bells = []
        for pair in range(BASIS // 2):
            center = jnp.where(upper, (2 * pair + 1) / (BASIS - 1), 2 * pair / (BASIS - 1))
            gap = squared - center
            gaps.append(gap)
            bells.append(jnp.exp(-basis_sharpness * (gap * gap)))
        sx, sy, sz = scaled
        angular = [
            None,
            root_three * sx,
            root_three * sy,
            root_three * sz,
            root_fifteen * sx * sy,
            root_fifteen * sy * sz,
            0.5 * root_five * (3.0 * sz * sz - squared),
            root_fifteen * sx * sz,
            0.5 * root_fifteen * (sx * sx - sy * sy),
        ]
        return scaled, mask, fade, gaps, bells, angular

    def forward(number, carry):
        target = pairs_ref[0, 0, 0, number]
        source = pairs_ref[0, 0, 1, number]
        last, place = carry
        fresh = source != last
        place = jnp.where(fresh, place + 1, place)

        @pl.when(fresh)
        def _():
            right = hu_tab[source, 0:TILE, :].astype(F32)
            for degree in range(3):
                for basis in range(BASIS):
                    hw[place, degree, basis * TILE : (basis + 1) * TILE, :] = (
                        wrad_ref[degree, basis : basis + 1, :] * right
                    ).astype(BF16)

        height = 16
        for first in range(0, TILE, height):
            scaled, mask, fade, gaps, bells, angular = scene(target, source, first, height)
            envelope = mask * (fade * fade * fade)
            for pair in range(BASIS // 2):
                radial = envelope * bells[pair]
                for order in range(ORDERS):
                    value = radial if order == 0 else angular[order] * radial
                    gb[
                        number,
                        order * TILE + first : order * TILE + first + height,
                        pair * LANES : (pair + 1) * LANES,
                    ] = value.astype(BF16)
        start = pl.multiple_of(target * TILE, TILE)
        for degree, (low, high) in enumerate(degree_limits):
            part = nn(gb[number, low * TILE : high * TILE, :], hw[place, degree])
            for order in range(low, high):
                sums[order, pl.ds(start, TILE), :] += part[
                    (order - low) * TILE : (order - low + 1) * TILE, :
                ]
        return source, place

    lax.fori_loop(0, live, forward, (jnp.int32(-1), jnp.int32(-1)))

    for pull in pulls[1:]:
        pull.wait()
    for degree, (low, high) in enumerate(degree_limits):
        for order in range(low, high):
            mixed[order] = nn((message_scale * sums[order]).astype(BF16), wmix_ref[degree])

    step = 16

    def squares(here):
        first_sq = sum(mixed[order, here, :] * mixed[order, here, :] for order in range(2, 4))
        first_sq = first_sq + mixed[1, here, :] * mixed[1, here, :]
        return first_sq

    def products(block, carry):
        here = pl.ds(pl.multiple_of(block * step, step), step)
        scalar = mixed[0, here, :]
        first_sq = squares(here)
        second_sq = mixed[4, here, :] * mixed[4, here, :]
        for order in range(5, 9):
            second_sq = second_sq + mixed[order, here, :] * mixed[order, here, :]
        prods[0, here, :] = scalar.astype(BF16)
        prods[1, here, :] = first_sq.astype(BF16)
        prods[2, here, :] = second_sq.astype(BF16)
        prods[3, here, :] = (scalar * first_sq).astype(BF16)
        return carry

    lax.fori_loop(0, rows // step, products, 0)
    message = nn(prods[0], wprod_ref[0])
    for part in range(1, 4):
        message = message + nn(prods[part], wprod_ref[part])
    sums[0] = message
    read = wread_ref[...]

    def gates(block, carry):
        here = pl.ds(pl.multiple_of(block * step, step), step)
        value = sums[0, here, :]
        gate = jax.nn.sigmoid(value)
        atom = lax.broadcasted_iota(jnp.int32, (step, channels), 0) + block * step
        weight = jnp.where(atom < count, read, 0.0)
        prods[0, here, :] = (weight * gate * (1.0 + value * (1.0 - gate))).astype(BF16)
        silu = value * gate * read
        top = silu.astype(BF16)
        prods[1, here, :] = top
        prods[2, here, :] = (silu - top.astype(F32)).astype(BF16)
        return carry

    lax.fori_loop(0, rows // step, gates, 0)
    ones = jnp.ones((8, channels), BF16)
    readout = (nt(ones, prods[1]) + nt(ones, prods[2]))[0:1, :]
    species = species_ref[0]
    reference_part = jnp.where(species == 0, eref_ref[0], eref_ref[1])
    atom_row = lax.broadcasted_iota(jnp.int32, (1, rows), 1)
    energy_ref[0] = jnp.where(atom_row < count, reference_part + readout, 0.0)
    for part in range(4):
        gprod[part] = nt(prods[0], wprod_ref[part])

    def unmix(block, carry):
        here = pl.ds(pl.multiple_of(block * step, step), step)
        scalar = mixed[0, here, :]
        last = gprod[3, here, :]
        gmix[0, here, :] = (gprod[0, here, :] + last * squares(here)).astype(BF16)
        factor = gprod[1, here, :] + last * scalar
        for order in range(1, 4):
            gmix[order, here, :] = (2.0 * mixed[order, here, :] * factor).astype(BF16)
        factor = gprod[2, here, :]
        for order in range(4, 9):
            gmix[order, here, :] = (2.0 * mixed[order, here, :] * factor).astype(BF16)
        return carry

    lax.fori_loop(0, rows // step, unmix, 0)
    for degree, (low, high) in enumerate(degree_limits):
        for order in range(low, high):
            back = (message_scale * nt(gmix[order], wmix_ref[degree])).astype(BF16)
            for tile in range(own_tiles):
                gat[tile, order * TILE : (order + 1) * TILE, :] = back[
                    tile * TILE : (tile + 1) * TILE, :
                ]

    def backward(number, carry):
        target = pairs_ref[0, 0, 0, number]
        source = pairs_ref[0, 0, 1, number]
        last, place = carry
        place = jnp.where(source != last, place + 1, place)
        gather = jnp.zeros((TILE, channels), F32)
        for degree, (low, high) in enumerate(degree_limits):
            grads = gat[target, low * TILE : high * TILE, :]
            gg[low * TILE : high * TILE, :] = nt(grads, hw[place, degree])
            held = tn(gb[number, low * TILE : high * TILE, :], grads)
            for basis in range(BASIS):
                gather = gather + (
                    wrad_ref[degree, basis : basis + 1, :]
                    * held[basis * TILE : (basis + 1) * TILE, :]
                )
        ghu[source] += gather
        height = 8
        totals = [jnp.zeros((height, LANES), F32) for axis in range(3)]
        for first in range(0, TILE, height):
            scaled, mask, fade, gaps, bells, angular = scene(target, source, first, height)
            sx, sy, sz = scaled
            fade_sq = mask * (fade * fade)
            envelope = fade_sq * fade
            d_angular = [None] * ORDERS
            d_squared = None
            for pair in range(BASIS // 2):
                radial = envelope * bells[pair]
                d_radial = None
                for order in range(ORDERS):
                    grad = gg[
                        order * TILE + first : order * TILE + first + height,
                        pair * LANES : (pair + 1) * LANES,
                    ]
                    if order == 0:
                        d_radial = grad
                        continue
                    d_radial = d_radial + grad * angular[order]
                    term = grad * radial
                    d_angular[order] = term if pair == 0 else d_angular[order] + term
                term = (
                    d_radial
                    * bells[pair]
                    * (-3.0 - (2.0 * basis_sharpness) * (fade * gaps[pair]))
                )
                d_squared = term if pair == 0 else d_squared + term
            d_squared = d_squared * fade_sq - (0.5 * root_five) * d_angular[6]
            twice = 2.0 * d_squared
            d_x = (
                root_three * d_angular[1]
                + root_fifteen * (sy * d_angular[4] + sz * d_angular[7] + sx * d_angular[8])
                + sx * twice
            )
            d_y = (
                root_three * d_angular[2]
                + root_fifteen * (sx * d_angular[4] + sz * d_angular[5] - sy * d_angular[8])
                + sy * twice
            )
            d_z = (
                root_three * d_angular[3]
                + root_fifteen * (sy * d_angular[5] + sx * d_angular[7])
                + sz * (twice + (3.0 * root_five) * d_angular[6])
            )
            here = pl.ds(pl.multiple_of(target * TILE + first, 8), height)
            for axis, value in enumerate((d_x, d_y, d_z)):
                gpl[axis, here, :] += value
                totals[axis] = totals[axis] + value
        for axis in range(3):
            gpr[source, axis] += totals[axis]
        return source, place

    lax.fori_loop(0, live, backward, (jnp.int32(-1), jnp.int32(-1)))

    def folded(tile, axis):
        line = jnp.sum(gpr[tile, axis], axis=0, keepdims=True)
        return (line + pltpu.roll(line, TILE, 1)) * (1.0 / cutoff_radius)

    ones = jnp.ones((8, LANES), BF16)
    for axis in range(3):
        lefts = gpl[axis]
        top = lefts.astype(BF16)
        rest = (lefts - top.astype(F32)).astype(BF16)
        line = (nt(ones, top) + nt(ones, rest))[0:1, :] * (1.0 / cutoff_radius)
        rights = []
        for tile in range(0, own_tiles, 2):
            rights.append(jnp.where(upper, folded(tile + 1, axis), folded(tile, axis)))
        own_pos_ref[axis : axis + 1, :] = jnp.concatenate(rights, axis=1) - line
    own_pos_ref[3:8, :] = jnp.zeros((5, rows), F32)
    for tile in range(own_tiles):
        own_hu_ref[tile * TILE : (tile + 1) * TILE, :] = ghu[tile]
    for number in range(cells):
        msg_ref[number, 0:TILE, :] = ghu[own_tiles + number].astype(BF16)
        lines = [folded(own_tiles + number, axis) for axis in range(3)]
        tops = [line.astype(BF16).astype(F32) for line in lines]
        rests = [line - top for line, top in zip(lines, tops)]
        packed = stack_rows(tops + rests, EXTRA, LANES)
        fill = jnp.zeros((EXTRA, channels - LANES), F32)
        msg_ref[number, TILE : TILE + EXTRA, :] = jnp.concatenate([packed, fill], axis=1).astype(BF16)


def vmem():
    return pl.BlockSpec(memory_space=pltpu.VMEM)


def hbm():
    return pl.BlockSpec(memory_space=pltpu.HBM)


def smem():
    return pl.BlockSpec(memory_space=pltpu.SMEM)


def body(
    nx,
    ny,
    positions,
    features,
    species,
    atom_count,
    quad_list,
    tile_pairs,
    w_up,
    w_radial,
    w_mix,
    w_prod,
    w_read,
    e_ref,
):
    rows = features.shape[2]
    channels = features.shape[3]
    cells = len(CELLS)
    own_tiles = rows // TILE
    tiles = own_tiles + cells
    max_pairs = tile_pairs.shape[2]
    block = TILE + EXTRA
    table, own_geo, own_cols = pl.pallas_call(
        functools.partial(halo_kernel, nx, ny),
        out_shape=(
            jax.ShapeDtypeStruct((tiles, block, channels), BF16),
            jax.ShapeDtypeStruct((own_tiles, 8, LANES), F32),
            jax.ShapeDtypeStruct((3, rows, LANES), F32),
        ),
        in_specs=[smem()] + [hbm()] * 4,
        out_specs=(vmem(), vmem(), vmem()),
        scratch_shapes=[
            pltpu.VMEM((4, block, channels), BF16),
            pltpu.VMEM(positions.shape, F32),
            pltpu.VMEM(features.shape, BF16),
            pltpu.VMEM(quad_list.shape, jnp.int32),
            pltpu.VMEM(w_up.shape, BF16),
            pltpu.SemaphoreType.DMA((4,)),
            pltpu.SemaphoreType.DMA((cells,)),
            pltpu.SemaphoreType.DMA((cells,)),
        ],
        compiler_params=pltpu.CompilerParams(
            collective_id=0, has_side_effects=True, vmem_limit_bytes=6 * 1024 * 1024
        ),
        cost_estimate=pl.CostEstimate(flops=4 * 10**9, bytes_accessed=32 * 1024 * 1024, transcendentals=0),
        name="halo",
    )(atom_count, positions, features, quad_list, w_up)
    energies, messages, grad_hu, grad_pos = pl.pallas_call(
        core_kernel,
        out_shape=(
            jax.ShapeDtypeStruct((1, 1, rows), F32),
            jax.ShapeDtypeStruct((cells, block, channels), BF16),
            jax.ShapeDtypeStruct((rows, channels), F32),
            jax.ShapeDtypeStruct((8, rows), F32),
        ),
        in_specs=[smem(), smem()] + [hbm()] * 3 + [vmem()] * 6,
        out_specs=(vmem(), vmem(), vmem(), vmem()),
        scratch_shapes=[
            pltpu.SMEM((1, 1, 2, max_pairs), jnp.int32),
            pltpu.VMEM(w_mix.shape, BF16),
            pltpu.VMEM(w_prod.shape, BF16),
            pltpu.SemaphoreType.DMA((3,)),
            pltpu.VMEM((tiles, 8, LANES), F32),
            pltpu.VMEM((max_pairs, 3, BASIS * TILE, channels), BF16),
            pltpu.VMEM((max_pairs, ORDERS * TILE, BASIS * TILE), BF16),
            pltpu.VMEM((ORDERS, rows, channels), F32),
            pltpu.VMEM((ORDERS, rows, channels), F32),
            pltpu.VMEM((4, rows, channels), BF16),
            pltpu.VMEM((4, rows, channels), F32),
            pltpu.VMEM((ORDERS, rows, channels), BF16),
            pltpu.VMEM((own_tiles, ORDERS * TILE, channels), BF16),
            pltpu.VMEM((ORDERS * TILE, BASIS * TILE), F32),
            pltpu.VMEM((tiles, TILE, channels), F32),
            pltpu.VMEM((tiles, 3, 8, LANES), F32),
            pltpu.VMEM((3, rows, LANES), F32),
        ],
        compiler_params=pltpu.CompilerParams(vmem_limit_bytes=40 * 1024 * 1024),
        name="core",
    )(
        atom_count,
        e_ref,
        jnp.swapaxes(tile_pairs, 2, 3),
        w_mix,
        w_prod,
        species,
        table,
        own_geo,
        own_cols,
        jnp.swapaxes(w_radial, 0, 1),
        w_read.reshape(1, channels),
    )
    total, shifts = pl.pallas_call(
        functools.partial(return_kernel, nx, ny),
        out_shape=(
            jax.ShapeDtypeStruct((rows, channels), BF16),
            jax.ShapeDtypeStruct((8, rows), F32),
        ),
        in_specs=[vmem()] * 4,
        out_specs=(vmem(), vmem()),
        scratch_shapes=[
            pltpu.VMEM((cells, block, channels), BF16),
            pltpu.VMEM((4, block, channels), BF16),
            pltpu.VMEM((rows, channels), F32),
            pltpu.SemaphoreType.DMA((cells,)),
            pltpu.SemaphoreType.DMA((cells,)),
        ],
        compiler_params=pltpu.CompilerParams(
            collective_id=1, has_side_effects=True, vmem_limit_bytes=8 * 1024 * 1024
        ),
        name="giveback",
    )(messages, grad_hu, grad_pos, quad_list)
    forces, feature_grad = pl.pallas_call(
        finish_kernel,
        out_shape=(
            jax.ShapeDtypeStruct((3, 1, 1, rows), F32),
            jax.ShapeDtypeStruct((1, 1, rows, channels), F32),
        ),
        in_specs=[vmem()] * 3,
        out_specs=(vmem(), vmem()),
        compiler_params=pltpu.CompilerParams(vmem_limit_bytes=4 * 1024 * 1024),
        name="finish",
    )(total, shifts, w_up)
    return (energies, forces, feature_grad)


def solution(mesh):
    placed = (
        P(None, "gx", "gy", None),
        P("gx", "gy", None, None),
        P("gx", "gy", None),
        P("gx", "gy"),
        P("gx", "gy", None, None, None),
        P("gx", "gy", None, None),
        P(),
        P(),
        P(),
        P(),
        P(),
        P(),
    )
    return jax.shard_map(
        functools.partial(body, mesh.shape["gx"], mesh.shape["gy"]),
        mesh=mesh,
        in_specs=placed,
        out_specs=(P("gx", "gy", None), P(None, "gx", "gy", None), P("gx", "gy", None, None)),
        check_vma=False,
    )
```
